32 devices in a mesh: req: 16 (over z, y, x), tp: 2 (over core).
Axes of the slice: x: 2, y: 2, z: 4, core: 2. Of those that a mesh axis runs over, the one named last changes fastest.
Arguments:
- attn: bfloat16 [2048, 2048], P('req', 'tp'), may hold values from -6 to 6
- out_weight: bfloat16 [2048, 2048], P('tp'), may hold values from -0.125 to 0.125
- stream_in: bfloat16 [2048, 2048], P(('req', 'tp')), may hold values from -12 to 12
- norm_gain: float32 [2048], replicated, may hold values from 0.5 to 1.5
- router_weight: bfloat16 [2048, 32], replicated, may hold values from -0.024902344 to 0.024902344
- routes: int32 [2048, 8], P(('req', 'tp')), may hold values from 0 to 31, all different within a row; in each aligned block of 64 rows (0 to 63, 64 to 127, ...) at most 32 rows name the same one
- gate_weight: bfloat16 [32, 1024, 2048], P('req', 'tp'), may hold values from -0.125 to 0.125
- up_weight: bfloat16 [32, 1024, 2048], P('req', 'tp'), may hold values from -0.125 to 0.125
- down_weight: bfloat16 [32, 1024, 2048], P('req', 'tp'), may hold values from -0.1875 to 0.1875
Outputs:
- stream: bfloat16 [2048, 2048], P(('req', 'tp'))
- expert_mix: bfloat16 [2048, 2048], P(('req', 'tp'))
The draws below stay inside these ranges and needn't reach their ends.
Inputs may be any that keep to these rules, and one draw needn't show every extreme that they name: `routes`: each row names 8 different experts; among the rows of one aligned block of 64 rows no expert is named by more than 32 rows, and some expert reaches 32 in some block.
All inputs are finite; a program needn't handle non-finite values.
Results may differ from the reference program's by a relative error of at most 0.009.
Values may be sent and summed in bfloat16 or wider, within the bound.
No kernel may reach another device: no remote copies, remote signals or barrier semaphores. Data moves between devices by JAX's collectives and lax.ppermute only.
A program may use at most 128 MiB of HBM per device.

```python
import math
import jax
import jax.numpy as jnp
import numpy as np
from jax import lax

D = 2048
HEADS = 16
HD = 128
FF = 1024
TOPK = 8
EXPERTS = 32
TOKENS = 2048
ROWS = 64
CAP = 32
N_REQ = 16
N_TP = 2


def draw_stream_in(key, part):
    key_base = jax.random.fold_in(key, 11)
    key_cols = jax.random.fold_in(key, 12)
    columns = jnp.exp(jax.random.uniform(key_cols, (D,), jnp.float32, math.log(0.3), math.log(3.0)))
    base = jnp.clip(jax.random.normal(key_base, (TOKENS, D), jnp.float32), -4.0, 4.0)
    return (base * columns[None, :]).astype(jnp.bfloat16)


def shard_levels(stream_key, shape, cuts, least, largest):
    level, own = 1.0, jax.random.fold_in(stream_key, 6)
    for position, parts in cuts:
        steps = jnp.exp(jax.random.uniform(jax.random.fold_in(own, position), (parts,), jnp.float32, least / len(cuts), largest / len(cuts)))
        level = level * jnp.repeat(steps, shape[position] // parts).reshape([-1 if axis == position else 1 for axis in range(len(shape))])
    return level


def deal_out(own_key, own, number, rows, amount, top, bound, slope):
    order = jax.random.permutation(own_key, amount)
    crowded, usual = portions_of(amount, rows * top, bound, slope, True), portions_of(amount, rows * top, bound, slope, False)
    places = jnp.arange(amount)

    def named(sizes, offset_by):
        used = int((sizes > 0).sum())
        fixed = max(1, used // 4)
        passed = fixed + (places - fixed + offset_by * (used - fixed)) % max(1, amount - fixed)
        return jnp.zeros((amount,), jnp.int32).at[order[jnp.where(places < fixed, places, passed)]].set(jnp.asarray(sizes, jnp.int32))

    sizes = jnp.where(number % 4 == 0, named(crowded, number // 4), named(usual, number - number // 4 - 1))
    mixed = jax.random.permutation(jax.random.fold_in(own, 3), amount)
    donor, sink = mixed[0:amount // 2 * 2:2], mixed[1:amount // 2 * 2:2]
    margin = jnp.minimum(sizes[donor] - 1, bound - sizes[sink]) // 2
    margin = jnp.where((donor == order[0]) | (sink == order[0]) | (sizes[sink] == 0), 0, jnp.maximum(margin, 0))
    passed = jax.random.randint(jax.random.fold_in(own, 4), (amount // 2,), 0, 1 << 20) % (margin + 1)
    sizes = sizes.at[donor].add(-passed).at[sink].add(passed)
    members = jnp.searchsorted(jnp.cumsum(sizes), jnp.arange(rows * top), side="right").astype(jnp.int32)
    listing = members.reshape(top, rows).T
    listing = listing[jax.random.permutation(jax.random.fold_in(own, 1), rows)]
    offset_by = jax.random.randint(jax.random.fold_in(own, 2), (rows, 1), 0, top)
    return jnp.take_along_axis(listing, (jnp.arange(top)[None, :] + offset_by) % top, axis=1)


def portions_of(count, total, limit, slope, full):
    portions = [(1 << 20) // math.isqrt(grade ** slope) + 1 for grade in range(1, count + 1)]
    largest = limit if full else min(limit, max(-(-total // count), total * portions[0] // sum(portions)))
    least = 1 if total - largest >= count - 1 else 0
    counts, surplus = [largest] + [least] * (count - 1), total - largest - least * (count - 1)
    while surplus > 0:
        free = [i for i in range(1, count) if counts[i] < largest] or [i for i in range(1, count) if counts[i] < limit]
        mass, left = sum([portions[i] for i in free]), surplus
        for i in free:
            more = min(limit - counts[i], max(1, left * portions[i] // mass), surplus)
            counts[i] = counts[i] + more
            surplus = surplus - more
    return np.array(counts)


def noise(rng, shape, width, limit, cuts=(), held_as=jnp.bfloat16):
    result = width * jax.random.normal(rng, shape, jnp.float32)
    if cuts:
        result = result * shard_levels(rng, shape, cuts, -0.22, 0.18)
    return jnp.clip(result, -limit, limit).astype(held_as)


def setup_inputs(seed: int = 0) -> dict:
    arg_keys = jax.random.split(jax.random.key(seed), 10)
    attn = noise(arg_keys[0], (TOKENS, HEADS * HD), 1.0, 6.0, ((0, 16), (1, 2)))
    out_weight = noise(arg_keys[1], (HEADS * HD, D), (HEADS * HD) ** -0.5, 0.125, ((0, 2),))
    stream_in = draw_stream_in(jax.random.fold_in(arg_keys[9], 71), 0)
    norm_gain = jnp.clip(1.0 + 0.1 * jax.random.normal(arg_keys[3], (D,), jnp.float32), 0.5, 1.5)
    router_weight = jnp.clip(jax.random.uniform(arg_keys[4], (D, EXPERTS), jnp.float32, -0.024902344, 0.024902344), -0.024902344, 0.024902344).astype(jnp.bfloat16)
    routes_keys = jax.random.split(jax.random.fold_in(arg_keys[5], 1), TOKENS // ROWS)
    routes_turns = jax.random.permutation(jax.random.fold_in(arg_keys[5], 3), TOKENS // ROWS)
    routes = jax.vmap(lambda own, number: deal_out(jax.random.fold_in(arg_keys[5], 2), own, number, ROWS, EXPERTS, TOPK, CAP, 2))(routes_keys, routes_turns).reshape((TOKENS, TOPK))
    gate_weight = noise(arg_keys[6], (EXPERTS, FF, D), D ** -0.5, 0.125, ((0, 16), (1, 2)))
    up_weight = noise(arg_keys[7], (EXPERTS, FF, D), D ** -0.5, 0.125, ((0, 16), (1, 2)))
    down_weight = noise(arg_keys[8], (EXPERTS, FF, D), FF ** -0.5, 0.1875, ((0, 16), (1, 2)))
    return {"attn": attn, "out_weight": out_weight, "stream_in": stream_in, "norm_gain": norm_gain, "router_weight": router_weight, "routes": routes, "gate_weight": gate_weight, "up_weight": up_weight, "down_weight": down_weight}


def slot_numbers(flat, count):
    onehot = (flat[:, None] == jnp.arange(count, dtype=jnp.int32)[None, :]).astype(jnp.int32)
    before = jnp.cumsum(onehot, axis=0) - onehot
    return lax.optimization_barrier(jnp.sum(before * onehot, axis=1)).astype(jnp.int32)

def reference(attn, out_weight, stream_in, norm_gain, router_weight, routes, gate_weight, up_weight, down_weight):
    proj = jnp.dot(attn, out_weight, preferred_element_type=jnp.float32)
    hidden_state = stream_in.astype(jnp.float32) + proj
    scale = lax.rsqrt(lax.optimization_barrier(jnp.mean(hidden_state * hidden_state, axis=1, keepdims=True)) + 1e-06)
    normed = (hidden_state * scale * norm_gain).astype(jnp.bfloat16)
    logits = jnp.dot(normed, router_weight, preferred_element_type=jnp.float32)
    onehot = (routes[:, :, None] == jnp.arange(EXPERTS, dtype=jnp.int32)[None, None, :]).astype(jnp.float32)
    picked = lax.optimization_barrier(jnp.sum(onehot * logits[:, None, :], axis=2))
    raised = jnp.exp(picked)
    gates = raised / lax.optimization_barrier(jnp.sum(raised, axis=1, keepdims=True))
    blocks = N_REQ * N_TP
    flat = routes.reshape(blocks, ROWS * TOPK)
    slots = jax.vmap(lambda f: slot_numbers(f, EXPERTS))(flat)
    anchor = jnp.arange(blocks, dtype=jnp.int32)[:, None] * CAP
    dest = (flat * (blocks * CAP) + anchor + slots).reshape(-1).astype(jnp.int32)
    source = (jnp.arange(TOKENS * TOPK, dtype=jnp.int32) // TOPK).astype(jnp.int32)
    buffer = jnp.zeros((EXPERTS * blocks * CAP, D), normed.dtype).at[dest].set(normed[source])
    buffer = buffer.reshape(EXPERTS, blocks * CAP, D)

    def one_expert(items):
        rows_in, gate_w, up_w, down_w = items
        gate_h = jnp.dot(rows_in, gate_w.T, preferred_element_type=jnp.float32)
        up_h = jnp.dot(rows_in, up_w.T, preferred_element_type=jnp.float32)
        act = (jax.nn.silu(gate_h) * up_h).astype(jnp.bfloat16)
        return jnp.dot(act, down_w, preferred_element_type=jnp.float32).astype(jnp.bfloat16)
    outputs = lax.map(one_expert, (buffer, gate_weight, up_weight, down_weight))
    expert_row = outputs.reshape(EXPERTS * blocks * CAP, D)[dest].reshape(TOKENS, TOPK, D)
    mix = lax.optimization_barrier(jnp.sum(gates[:, :, None] * expert_row.astype(jnp.float32), axis=1))
    return (hidden_state.astype(jnp.bfloat16), mix.astype(jnp.bfloat16))
```

```python
import functools

import jax
import jax.numpy as jnp
from jax import lax
from jax.experimental import pallas as pl
from jax.experimental.pallas import tpu as pltpu
from jax.sharding import PartitionSpec as P

SWAP = [(0, 1), (1, 0)]
PLACES = 16
ACROSS_X = [(i, i ^ 1) for i in range(PLACES)]
ACROSS_Y = [(i, i ^ 2) for i in range(PLACES)]
PAIR_Z = [(i, i ^ 4) for i in range(PLACES)]
MIDDLE_Z = [(i, i ^ 12) for i in range(4, 12)]
INWARD_Z = [(i, i ^ 4) for i in (0, 1, 2, 3, 12, 13, 14, 15)]
OUTWARD_Z = [(i, i ^ 4) for i in range(4, 12)]
NT = (((1,), (1,)), ((), ()))


def send(value, pairs):
    return lax.ppermute(value, "req", pairs)


def wide(value):
    return value.astype(jnp.float32)


def narrow(value):
    return value.astype(jnp.bfloat16)


def joined(*parts):
    return jnp.concatenate(parts, axis=0)


def spread(own):
    rows = own.shape[0]
    half = rows // 2
    z = lax.axis_index("req") // 4
    middle = (z == 1) | (z == 2)
    x0 = send(own, ACROSS_X)
    y0 = send(own, ACROSS_Y)
    pair = send(own, PAIR_Z)
    near = send(own, MIDDLE_Z)
    x1 = send(joined(pair, y0[:half]), ACROSS_X)
    y1 = send(joined(pair, x0[half:]), ACROSS_Y)
    near_out = send(near, OUTWARD_Z)
    next_ = send(pair, MIDDLE_Z)
    next_out = send(next_, OUTWARD_Z)
    far = joined(jnp.where(middle, near, near_out), jnp.where(middle, next_, next_out))
    x2 = send(joined(far, y1[:half]), ACROSS_X)
    y2 = send(joined(far, x1[half:rows]), ACROSS_Y)
    x3 = send(joined(y2[:half], y2[rows : rows + half]), ACROSS_X)
    y3 = send(joined(x2[half:rows], x2[rows + half : 2 * rows]), ACROSS_Y)
    return [own, x0, y0, pair, x1, y1], [far, x2, y2, x3, y3]


def collect(first, second):
    own, x0, y0, pair, x1, y1 = first
    far1, far2, x_far1, x_far2, y_far1, y_far2, x3, y3 = second
    rows = own.shape[0]
    half = rows // 2

    def low(value, term):
        return joined(narrow(wide(value[:half]) + wide(term)), value[half:])

    def high(value, term):
        return joined(
            value[:half], narrow(wide(value[half:rows]) + wide(term)), value[rows:]
        )

    by_x = send(x3, ACROSS_X)
    by_y = send(y3, ACROSS_Y)
    x_sum = send(high(x_far2, by_y[half:]), ACROSS_X)
    y_sum = send(low(y_far2, by_x[half:]), ACROSS_Y)
    far2 = narrow(wide(far2) + wide(x_sum) + wide(y_sum))
    far2 = narrow(wide(far2) + wide(send(far2, INWARD_Z)))
    next_ = send(far2, MIDDLE_Z)
    x_sum = send(high(x_far1, by_y[:half]), ACROSS_X)
    y_sum = send(low(y_far1, by_x[:half]), ACROSS_Y)
    far1 = narrow(wide(far1) + wide(x_sum[:rows]) + wide(y_sum[:rows]))
    far1 = narrow(wide(far1) + wide(send(far1, INWARD_Z)))
    near = send(far1, MIDDLE_Z)
    x_pair = send(high(x1, y_sum[rows:]), ACROSS_X)
    y_pair = send(low(y1, x_sum[rows:]), ACROSS_Y)
    pair = narrow(wide(pair) + wide(x_pair[:rows]) + wide(y_pair[:rows]) + wide(next_))
    by_pair = send(pair, PAIR_Z)
    x_own = send(high(x0, y_pair[rows:]), ACROSS_X)
    y_own = send(low(y0, x_pair[rows:]), ACROSS_Y)
    total = wide(own) + wide(x_own) + wide(y_own)
    return total + wide(near) + wide(by_pair)


def expert_body(takes, gives, chunks, tiles, *refs):
    blocks = refs[: len(takes)]
    router, local, gate_own, up_own, down_own, gate_far, up_far, down_far = refs[
        len(takes) : len(takes) + 8
    ]
    outs = refs[len(takes) + 8 : len(takes) + 8 + len(gives)]
    held, gates, total = refs[len(takes) + 8 + len(gives) :]
    width = held.shape[1]
    experts = router.shape[1]
    step = pl.program_id(0)

    @pl.when(step == 0)
    def _():
        at = 0
        for block, size in zip(blocks, takes):
            rows = block[:, :width]
            held[at : at + size, :] = rows
            chosen = block[:, width : width + experts]
            logits = jnp.dot(rows, router[...], preferred_element_type=jnp.float32)
            raised = jnp.where(chosen > 0, jnp.exp(logits), 0.0)
            gate = raised / jnp.sum(raised, axis=1, keepdims=True)
            for j in range(2):
                mine = jnp.sum(gate * local[j : j + 1, :], axis=1, keepdims=True)
                gates[j, at : at + size, :] = jnp.broadcast_to(mine, (size, 128))
            at += size

    expert = step // (tiles // 2)
    at = 0
    for size in chunks:
        part = slice(at, at + size)
        weight = gates[expert, part, :]
        x = held[part, :]
        out = None
        for gate_w, up_w, down_w in (
            (gate_own, up_own, down_own),
            (gate_far, up_far, down_far),
        ):
            h = lax.dot_general(x, gate_w[...], NT, preferred_element_type=jnp.float32)
            u = lax.dot_general(x, up_w[...], NT, preferred_element_type=jnp.float32)
            act = h / (1.0 + jnp.exp(-h)) * u
            act = act * jnp.concatenate([weight] * (act.shape[1] // 128), axis=1)
            term = jnp.dot(
                act.astype(jnp.bfloat16), down_w[...], preferred_element_type=jnp.float32
            )
            out = term if out is None else out + term

        @pl.when(step == 0)
        def _():
            total[part, :] = out

        @pl.when(step > 0)
        def _():
            total[part, :] += out

        at += size

    @pl.when(step == tiles - 1)
    def _():
        for out, ranges in zip(outs, gives):
            at = 0
            for start, size in ranges:
                out[at : at + size, :] = total[start : start + size, :].astype(jnp.bfloat16)
                at += size


def run_experts(blocks, takes, gives, chunks, router, local, own, far, tile):
    width = router.shape[0]
    hidden = own[0].shape[0] * own[0].shape[1]
    tiles = hidden // tile
    total_rows = sum(takes)
    whole = lambda shape: pl.BlockSpec(shape, lambda t: (0,) * len(shape))
    weight = pl.BlockSpec((tile, width), lambda t: (t, 0))
    flat = [w.reshape(hidden, width) for w in (*own, *far)]
    sizes = [sum(size for _, size in ranges) for ranges in gives]
    return pl.pallas_call(
        functools.partial(expert_body, takes, gives, chunks, tiles),
        grid=(tiles,),
        in_specs=[whole((size, blocks[0].shape[1])) for size in takes]
        + [whole(router.shape), whole(local.shape)]
        + [weight] * 6,
        out_specs=[whole((size, width)) for size in sizes],
        out_shape=[jax.ShapeDtypeStruct((size, width), jnp.bfloat16) for size in sizes],
        scratch_shapes=[
            pltpu.VMEM((total_rows, width), jnp.bfloat16),
            pltpu.VMEM((2, total_rows, 128), jnp.float32),
            pltpu.VMEM((total_rows, width), jnp.float32),
        ],
        compiler_params=pltpu.CompilerParams(vmem_limit_bytes=48 * 1024 * 1024),
        cost_estimate=pl.CostEstimate(
            flops=12 * total_rows * width * hidden,
            bytes_accessed=12 * hidden * width + 4 * total_rows * width,
            transcendentals=2 * total_rows * hidden,
        ),
    )(*blocks, router, local, *flat)


def project(attn, out_weight, stream_in):
    rows = stream_in.shape[0]
    me = lax.axis_index("tp")
    theirs = lax.dynamic_slice_in_dim(attn, (1 - me) * rows, rows, 0)
    ours = lax.dynamic_slice_in_dim(attn, me * rows, rows, 0)
    sent = jnp.dot(theirs, out_weight, preferred_element_type=jnp.float32)
    got = lax.ppermute(sent, "tp", SWAP)
    kept = jnp.dot(ours, out_weight, preferred_element_type=jnp.float32)
    return stream_in.astype(jnp.float32) + (kept + got)


def on_places(
    attn, out_weight, stream_in, norm_gain, router_weight, routes, gate_weight, up_weight, down_weight
):
    rows = stream_in.shape[0]
    half = rows // 2
    expert_count = router_weight.shape[1]
    experts = jnp.arange(expert_count, dtype=jnp.int32)
    me = lax.axis_index("req")
    named = jnp.any(routes[:, :, None] == experts, axis=1).astype(jnp.bfloat16)
    named = jnp.pad(named, ((0, 0), (0, 128 - expert_count)))
    local = (experts[None, :] == 2 * me + jnp.arange(2, dtype=jnp.int32)[:, None]).astype(
        jnp.float32
    )
    hidden_state = project(attn, out_weight, stream_in)
    scale = lax.rsqrt(jnp.mean(hidden_state * hidden_state, axis=1, keepdims=True) + 1e-06)
    normed = (hidden_state * scale * norm_gain).astype(jnp.bfloat16)
    own = (gate_weight, up_weight, down_weight)
    far = tuple(lax.ppermute(w, "tp", SWAP) for w in own)
    first, second = spread(jnp.concatenate([normed, named], axis=1))
    run = functools.partial(
        run_experts, router=router_weight, local=local, own=own, far=far, tile=256
    )
    takes = (rows, rows, rows, rows, rows + half, rows + half)
    starts = [sum(takes[:i]) for i in range(len(takes))]
    gives = tuple(((start, size),) for start, size in zip(starts, takes))
    chunks = (sum(takes) // 2,) * 2
    first = run(first, takes, gives, chunks)
    takes = (2 * rows, 2 * rows + half, 2 * rows + half, rows, rows)
    starts = [sum(takes[:i]) for i in range(len(takes))]
    gives = (
        ((0, rows),),
        ((rows, rows),),
        ((starts[1], rows), (starts[1] + 2 * rows, half)),
        ((starts[1] + rows, rows),),
        ((starts[2], rows), (starts[2] + 2 * rows, half)),
        ((starts[2] + rows, rows),),
        ((starts[3], rows),),
        ((starts[4], rows),),
    )
    chunks = (sum(takes) // 2,) * 2
    second = run(second, takes, gives, chunks)
    mix = collect(first, second)
    return (hidden_state.astype(jnp.bfloat16), mix.astype(jnp.bfloat16))


def slot_numbers(flat, count):
    onehot = (flat[:, None] == jnp.arange(count, dtype=jnp.int32)[None, :]).astype(jnp.int32)
    before = jnp.cumsum(onehot, axis=0) - onehot
    return jnp.sum(before * onehot, axis=1)


def swiglu_part(rows_in, gate_w, up_w, down_w):
    gate_h = jnp.einsum("ekd,efd->ekf", rows_in, gate_w, preferred_element_type=jnp.float32)
    up_h = jnp.einsum("ekd,efd->ekf", rows_in, up_w, preferred_element_type=jnp.float32)
    act = (jax.nn.silu(gate_h) * up_h).astype(jnp.bfloat16)
    return jnp.einsum("ekf,efd->ekd", act, down_w, preferred_element_type=jnp.float32)


def on_slots(
    attn, out_weight, stream_in, norm_gain, router_weight, routes, gate_weight, up_weight, down_weight
):
    rows, width = stream_in.shape
    hidden_state = project(attn, out_weight, stream_in)
    scale = lax.rsqrt(jnp.mean(hidden_state * hidden_state, axis=1, keepdims=True) + 1e-06)
    normed = (hidden_state * scale * norm_gain).astype(jnp.bfloat16)
    expert_count = router_weight.shape[1]
    choose_count = routes.shape[1]
    local_experts = gate_weight.shape[0]
    req_count = lax.axis_size("req")
    capacity = 2 * rows * choose_count // expert_count
    logits = jnp.dot(normed, router_weight, preferred_element_type=jnp.float32)
    onehot = (
        routes[:, :, None] == jnp.arange(expert_count, dtype=jnp.int32)[None, None, :]
    ).astype(jnp.float32)
    picked = jnp.sum(onehot * logits[:, None, :], axis=2)
    raised = jnp.exp(picked)
    gates = raised / jnp.sum(raised, axis=1, keepdims=True)
    flat = routes.reshape(-1)
    slots = slot_numbers(flat, expert_count)
    position = (
        flat % local_experts * (req_count * capacity) + flat // local_experts * capacity + slots
    )
    source = jnp.arange(rows * choose_count, dtype=jnp.int32) // choose_count
    outgoing = (
        jnp.zeros((local_experts * req_count * capacity, width), jnp.bfloat16)
        .at[position]
        .set(normed[source])
    )
    outgoing = outgoing.reshape(local_experts, req_count * capacity, width)
    incoming = lax.all_to_all(outgoing, "req", split_axis=1, concat_axis=1, tiled=True)
    partial_out = swiglu_part(
        lax.all_gather(incoming, "tp", axis=1, tiled=True), gate_weight, up_weight, down_weight
    )
    expert_out = lax.psum_scatter(partial_out, "tp", scatter_dimension=1, tiled=True).astype(
        jnp.bfloat16
    )
    returned = lax.all_to_all(expert_out, "req", split_axis=1, concat_axis=1, tiled=True)
    expert_row = returned.reshape(-1, width)[position].reshape(rows, choose_count, width)
    mix = jnp.einsum("rk,rkd->rd", gates, expert_row.astype(jnp.float32))
    return (hidden_state.astype(jnp.bfloat16), mix.astype(jnp.bfloat16))


def solution(mesh):
    body = on_places if mesh.shape["req"] == PLACES else on_slots
    return jax.shard_map(
        body,
        mesh=mesh,
        in_specs=(
            P("req", "tp"),
            P("tp", None),
            P(("req", "tp"), None),
            P(),
            P(),
            P(("req", "tp"), None),
            P("req", "tp", None),
            P("req", "tp", None),
            P("req", "tp", None),
        ),
        out_specs=(P(("req", "tp"), None), P(("req", "tp"), None)),
        check_vma=False,
    )
```

```python
import functools

import jax
import jax.numpy as jnp
from jax import lax
from jax.experimental import pallas as pl
from jax.experimental.pallas import tpu as pltpu
from jax.sharding import PartitionSpec as P

SWAP = [(0, 1), (1, 0)]
PLACES = 16
ACROSS_X = [(2 * i + t, 2 * (i ^ (1 + t)) + t) for i in range(PLACES) for t in range(2)]
ACROSS_Y = [(2 * i + t, 2 * (i ^ (2 - t)) + t) for i in range(PLACES) for t in range(2)]


def along_z(places):
    return [(2 * i + t, 2 * j + t) for i, j in places for t in range(2)]


PAIR_Z = along_z([(i, i ^ 4) for i in range(PLACES)])
MIDDLE_Z = along_z([(i, i ^ 12) for i in range(4, 12)])
OPPOSITE_Z = along_z([(i, i ^ 12) for i in range(PLACES)])
INWARD_Z = along_z([(i, i ^ 4) for i in (0, 1, 2, 3, 12, 13, 14, 15)])
OUTWARD_Z = along_z([(i, i ^ 4) for i in range(4, 12)])
NT = (((1,), (1,)), ((), ()))


def send(value, pairs):
    return lax.ppermute(value, ("req", "tp"), pairs)


def wide(value):
    return value.astype(jnp.float32)


def narrow(value):
    return value.astype(jnp.bfloat16)


def joined(*parts):
    return jnp.concatenate(parts, axis=0)


def together(*values):
    return lax.optimization_barrier(values)


def spread(own, weights):
    rows = own.shape[0]
    half = rows // 2
    z = lax.axis_index("req") // 4
    middle = (z == 1) | (z == 2)
    swapped = []

    def swap(value):
        swapped.append(lax.ppermute(value, "tp", SWAP))

    gate_w, up_w, down_w = weights
    swap(gate_w)
    own, up_w, swapped[0] = together(own, up_w, swapped[0])
    over = send(own, OPPOSITE_Z)
    pair = send(own, PAIR_Z)
    x0 = send(own, ACROSS_X)
    y0 = send(own, ACROSS_Y)
    swap(up_w)
    over, pair, x0, y0, swapped[1] = together(over, pair, x0, y0, swapped[1])
    to_x = joined(pair, y0[:half])
    to_y = joined(pair, x0[half:])
    over, pair, to_x, to_y, down_w = together(over, pair, to_x, to_y, down_w)
    out = send(over, OUTWARD_Z)
    next_ = send(pair, MIDDLE_Z)
    x1 = send(to_x, ACROSS_X)
    y1 = send(to_y, ACROSS_Y)
    swap(down_w)
    out, next_, x1, y1, swapped[2] = together(out, next_, x1, y1, swapped[2])
    far1 = jnp.where(middle, over, out)
    far2 = jnp.where(middle, next_, over)
    to_x = joined(far1, far2, y1[:half])
    to_y = joined(far1, far2, x1[half:rows])
    far1, far2, to_x, to_y = together(far1, far2, to_x, to_y)
    x2 = send(to_x, ACROSS_X)
    y2 = send(to_y, ACROSS_Y)
    return [own, x0, y0, pair, x1, y1], far1, far2, x2, y2, swapped


def spread_last(x2, y2, rows):
    half = rows // 2
    to_x = joined(y2[:half], y2[rows : rows + half])
    to_y = joined(x2[half:rows], x2[rows + half : 2 * rows])
    to_x, to_y = together(to_x, to_y)
    return send(to_x, ACROSS_X), send(to_y, ACROSS_Y)


def collect(first, second):
    own, x0, y0, pair, x1, y1 = first
    far1, far2, x_far1, x_far2, y_far1, y_far2, x3, y3 = second
    rows = own.shape[0]
    half = rows // 2

    def low(value, term):
        return joined(narrow(wide(value[:half]) + wide(term)), value[half:])

    def high(value, term):
        return joined(
            value[:half], narrow(wide(value[half:rows]) + wide(term)), value[rows:]
        )

    by_x = send(x3, ACROSS_X)
    by_y = send(y3, ACROSS_Y)
    x_sum = send(high(x_far2, by_y[half:]), ACROSS_X)
    y_sum = send(low(y_far2, by_x[half:]), ACROSS_Y)
    z = lax.axis_index("req") // 4
    middle = (z == 1) | (z == 2)
    far2 = wide(far2) + wide(x_sum) + wide(y_sum)
    next_ = send(narrow(far2), MIDDLE_Z)
    x_sum = send(high(x_far1, by_y[:half]), ACROSS_X)
    y_sum = send(low(y_far1, by_x[:half]), ACROSS_Y)
    far1 = wide(far1) + wide(x_sum[:rows]) + wide(y_sum[:rows])
    inward = send(narrow(far1), INWARD_Z)
    over = send(narrow(jnp.where(middle, far1 + wide(inward), far2)), OPPOSITE_Z)
    x_pair = send(high(x1, y_sum[rows:]), ACROSS_X)
    y_pair = send(low(y1, x_sum[rows:]), ACROSS_Y)
    pair = wide(pair) + wide(x_pair[:rows]) + wide(y_pair[:rows])
    by_pair = send(narrow(pair + wide(next_)), PAIR_Z)
    x_own = send(high(x0, y_pair[rows:]), ACROSS_X)
    y_own = send(low(y0, x_pair[rows:]), ACROSS_Y)
    total = wide(own) + wide(x_own) + wide(y_own)
    return total + wide(over) + wide(by_pair)


def expert_body(takes, gives, tile, group, *refs):
    pieces = len({i for i, _, _ in takes})
    blocks = refs[:pieces]
    router, local, gate_own, up_own, down_own, gate_far, up_far, down_far = refs[
        pieces : pieces + 8
    ]
    outs = refs[pieces + 8 : pieces + 8 + len(gives)]
    held, picks, spreads, sel, acts, ups, downs, up_sem, down_sem = refs[
        pieces + 8 + len(gives) :
    ]
    total_rows, width = held.shape
    experts = router.shape[1]
    tiles = acts.shape[1]
    groups = total_rows // group
    slots = group // 2

    def up_copies(t):
        part = pl.ds(pl.multiple_of(t * tile, tile), tile)
        return [
            pltpu.make_async_copy(w.at[part, :], ups.at[i, t], up_sem.at[i, t])
            for i, w in enumerate((gate_own, up_own, gate_far, up_far))
        ]

    def down_copy(i):
        return pltpu.make_async_copy(
            (down_own, down_far)[i], downs.at[i], down_sem.at[i]
        )

    for t in range(min(2, tiles)):
        for copy in up_copies(t):
            copy.start()
    at = 0
    for i, start, size in takes:
        held[at : at + size, :] = blocks[i][start : start + size, :width]
        picks[at : at + size, :] = blocks[i][start : start + size, width : width + 128]
        at += size
    for g in range(groups):
        part = slice(g * group, (g + 1) * group)
        x = held[part, :]
        pick = picks[part, :experts].astype(jnp.float32)
        logits = jnp.dot(x, router[...], preferred_element_type=jnp.float32)
        raised = jnp.where(pick > 0, jnp.exp(logits), 0.0)
        gate = raised / jnp.sum(raised, axis=1, keepdims=True)
        row = lax.broadcasted_iota(jnp.int32, (group, 1), 0)
        column = lax.broadcasted_iota(jnp.int32, (group, group), 1)
        chosen = jnp.zeros((group, group), jnp.float32)
        weighed = jnp.zeros((group, group), jnp.float32)
        for j in range(2):
            mine = local[j : j + 1, :]
            slot = jnp.sum(pick * mine, axis=1, keepdims=True).astype(jnp.int32)
            place = jnp.where(slot > 0, j * slots + row // 64 * 32 + slot - 1, -1)
            weight = jnp.sum(gate * mine, axis=1, keepdims=True)
            hit = column == place
            chosen = jnp.where(hit, 1.0, chosen)
            weighed = jnp.where(hit, weight, weighed)
        spreads[g] = weighed.astype(jnp.bfloat16)
        rows = jnp.dot(
            chosen.T.astype(jnp.bfloat16), x, preferred_element_type=jnp.float32
        ).astype(jnp.bfloat16)
        for j in range(2):
            sel[j, g * slots : (g + 1) * slots, :] = rows[j * slots : (j + 1) * slots, :]

    def up(t, _):
        @pl.when(t + 2 < tiles)
        def _():
            for copy in up_copies(t + 2):
                copy.start()

        @pl.when(t + 2 == tiles)
        def _():
            for i in range(2):
                down_copy(i).start()

        for copy in up_copies(t):
            copy.wait()
        x = sel[t // (tiles // 2)]
        for i in range(2):
            h = lax.dot_general(x, ups[2 * i, t], NT, preferred_element_type=jnp.float32)
            u = lax.dot_general(
                x, ups[2 * i + 1, t], NT, preferred_element_type=jnp.float32
            )
            acts[i, t] = (h / (1.0 + jnp.exp(-h)) * u).astype(jnp.bfloat16)
        return 0

    lax.fori_loop(0, tiles, up, 0)
    for i in range(2):
        down_copy(i).wait()

    def down(n, _):
        part = pl.ds(pl.multiple_of(n * tile, tile), tile)
        rows = []
        for j in range(2):
            total = None
            for t in range(j * tiles // 2, (j + 1) * tiles // 2):
                for i in range(2):
                    term = jnp.dot(
                        acts[i, t],
                        downs[i, t * tile : (t + 1) * tile, part],
                        preferred_element_type=jnp.float32,
                    )
                    total = term if total is None else total + term
            rows.append(total.astype(jnp.bfloat16))
        mixed = []
        for g in range(groups):
            slot_rows = jnp.concatenate(
                [r[g * slots : (g + 1) * slots, :] for r in rows], axis=0
            )
            mixed.append(
                jnp.dot(spreads[g], slot_rows, preferred_element_type=jnp.float32).astype(
                    jnp.bfloat16
                )
            )
        for out, ranges in zip(outs, gives):
            at = 0
            for start, size in ranges:
                g = start // group
                out[at : at + size, part] = mixed[g][start - g * group : start - g * group + size, :]
                at += size
        return 0

    lax.fori_loop(0, width // tile, down, 0)


def run_experts(blocks, takes, gives, router, local, own, far, tile=256, group=256):
    width = router.shape[0]
    hidden = own[0].shape[0]
    total_rows = sum(size for _, _, size in takes)
    sizes = [sum(size for _, size in ranges) for ranges in gives]
    vmem = pl.BlockSpec(memory_space=pltpu.VMEM)
    return pl.pallas_call(
        functools.partial(expert_body, takes, gives, tile, group),
        in_specs=[vmem] * (len(blocks) + 2) + [pl.BlockSpec(memory_space=pl.ANY)] * 6,
        out_specs=[vmem] * len(sizes),
        out_shape=[jax.ShapeDtypeStruct((size, width), jnp.bfloat16) for size in sizes],
        scratch_shapes=[
            pltpu.VMEM((total_rows, width), jnp.bfloat16),
            pltpu.VMEM((total_rows, 128), jnp.bfloat16),
            pltpu.VMEM((total_rows // group, group, group), jnp.bfloat16),
            pltpu.VMEM((2, total_rows // 2, width), jnp.bfloat16),
            pltpu.VMEM((2, hidden // tile, total_rows // 2, tile), jnp.bfloat16),
            pltpu.VMEM((4, hidden // tile, tile, width), jnp.bfloat16),
            pltpu.VMEM((2, hidden, width), jnp.bfloat16),
            pltpu.SemaphoreType.DMA((4, hidden // tile)),
            pltpu.SemaphoreType.DMA((2,)),
        ],
        compiler_params=pltpu.CompilerParams(vmem_limit_bytes=42 * 1024 * 1024),
        cost_estimate=pl.CostEstimate(
            flops=8 * total_rows * width * hidden,
            bytes_accessed=12 * hidden * width + 4 * total_rows * width,
            transcendentals=total_rows * hidden,
        ),
    )(*blocks, router, local, *own, *far)


def project(attn, out_weight, stream_in, later):
    rows = stream_in.shape[0]
    me = lax.axis_index("tp")
    theirs = lax.dynamic_slice_in_dim(attn, (1 - me) * rows, rows, 0)
    ours = lax.dynamic_slice_in_dim(attn, me * rows, rows, 0)
    sent = jnp.dot(theirs, out_weight, preferred_element_type=jnp.float32)
    got = lax.ppermute(sent, "tp", SWAP)
    kept = jnp.dot(ours, out_weight, preferred_element_type=jnp.float32)
    got, later = lax.optimization_barrier((got, later))
    return stream_in.astype(jnp.float32) + (kept + got), later


def on_places(
    attn, out_weight, stream_in, norm_gain, router_weight, routes, gate_weight, up_weight, down_weight
):
    rows = stream_in.shape[0]
    half = rows // 2
    expert_count = router_weight.shape[1]
    experts = jnp.arange(expert_count, dtype=jnp.int32)
    me = lax.axis_index("req")
    named = jnp.any(routes[:, :, None] == experts, axis=1).astype(jnp.bfloat16)
    order = jnp.arange(rows)
    earlier = (order[None, :] <= order[:, None]).astype(jnp.bfloat16)
    slot = jnp.dot(earlier, named, preferred_element_type=jnp.float32)
    slot = (slot * named).astype(jnp.bfloat16)
    slot = jnp.pad(slot, ((0, 0), (0, 128 - expert_count)))
    local = (experts[None, :] == 2 * me + jnp.arange(2, dtype=jnp.int32)[:, None]).astype(
        jnp.float32
    )
    hidden_state, gate_weight = project(attn, out_weight, stream_in, gate_weight)
    scale = lax.rsqrt(jnp.mean(hidden_state * hidden_state, axis=1, keepdims=True) + 1e-06)
    normed = (hidden_state * scale * norm_gain).astype(jnp.bfloat16)
    width = stream_in.shape[1]
    weights = (gate_weight, up_weight, down_weight)
    own = tuple(w.reshape(-1, width) for w in weights)
    first, far1, far2, x2, y2, far = spread(jnp.concatenate([normed, slot], axis=1), weights)
    far = tuple(w.reshape(-1, width) for w in far)
    run = functools.partial(run_experts, router=router_weight, local=local, own=own, far=far)
    takes = tuple((i, 0, rows) for i in range(7)) + ((4, rows, half), (5, rows, half))
    gives = tuple(((i * rows, rows),) for i in range(4))
    gives += (((4 * rows, rows), (7 * rows, half)),)
    gives += (((5 * rows, rows), (7 * rows + half, half)),)
    gives += (((6 * rows, rows),),)
    done = run(first + [far1], takes, gives)
    x2, y2, *done = lax.optimization_barrier((x2, y2, *done))
    x3, y3 = spread_last(x2, y2, rows)
    first, (far1,) = done[:6], done[6:]
    takes = ((0, 0, 2 * rows), (1, 0, 2 * rows), (0, 2 * rows, half), (1, 2 * rows, half))
    takes += ((2, 0, half), (3, 0, half), (2, half, half), (3, half, half), (4, 0, rows))
    gives = (
        ((0, rows), (4 * rows, half)),
        ((rows, rows),),
        ((2 * rows, rows), (4 * rows + half, half)),
        ((3 * rows, rows),),
        ((5 * rows, half), (6 * rows, half)),
        ((5 * rows + half, half), (6 * rows + half, half)),
        ((7 * rows, rows),),
    )
    *second, far2 = run([x2, y2, x3, y3, far2], takes, gives)
    second = [far1, far2, *second]
    mix = collect(first, second)
    return (hidden_state.astype(jnp.bfloat16), mix.astype(jnp.bfloat16))


def slot_numbers(flat, count):
    onehot = (flat[:, None] == jnp.arange(count, dtype=jnp.int32)[None, :]).astype(jnp.int32)
    before = jnp.cumsum(onehot, axis=0) - onehot
    return jnp.sum(before * onehot, axis=1)


def swiglu_part(rows_in, gate_w, up_w, down_w):
    gate_h = jnp.einsum("ekd,efd->ekf", rows_in, gate_w, preferred_element_type=jnp.float32)
    up_h = jnp.einsum("ekd,efd->ekf", rows_in, up_w, preferred_element_type=jnp.float32)
    act = (jax.nn.silu(gate_h) * up_h).astype(jnp.bfloat16)
    return jnp.einsum("ekf,efd->ekd", act, down_w, preferred_element_type=jnp.float32)


def on_slots(
    attn, out_weight, stream_in, norm_gain, router_weight, routes, gate_weight, up_weight, down_weight
):
    rows, width = stream_in.shape
    hidden_state, _ = project(attn, out_weight, stream_in, gate_weight)
    scale = lax.rsqrt(jnp.mean(hidden_state * hidden_state, axis=1, keepdims=True) + 1e-06)
    normed = (hidden_state * scale * norm_gain).astype(jnp.bfloat16)
    expert_count = router_weight.shape[1]
    choose_count = routes.shape[1]
    local_experts = gate_weight.shape[0]
    req_count = lax.axis_size("req")
    capacity = 2 * rows * choose_count // expert_count
    logits = jnp.dot(normed, router_weight, preferred_element_type=jnp.float32)
    onehot = (
        routes[:, :, None] == jnp.arange(expert_count, dtype=jnp.int32)[None, None, :]
    ).astype(jnp.float32)
    picked = jnp.sum(onehot * logits[:, None, :], axis=2)
    raised = jnp.exp(picked)
    gates = raised / jnp.sum(raised, axis=1, keepdims=True)
    flat = routes.reshape(-1)
    slots = slot_numbers(flat, expert_count)
    position = (
        flat % local_experts * (req_count * capacity) + flat // local_experts * capacity + slots
    )
    source = jnp.arange(rows * choose_count, dtype=jnp.int32) // choose_count
    outgoing = (
        jnp.zeros((local_experts * req_count * capacity, width), jnp.bfloat16)
        .at[position]
        .set(normed[source])
    )
    outgoing = outgoing.reshape(local_experts, req_count * capacity, width)
    incoming = lax.all_to_all(outgoing, "req", split_axis=1, concat_axis=1, tiled=True)
    partial_out = swiglu_part(
        lax.all_gather(incoming, "tp", axis=1, tiled=True), gate_weight, up_weight, down_weight
    )
    expert_out = lax.psum_scatter(partial_out, "tp", scatter_dimension=1, tiled=True).astype(
        jnp.bfloat16
    )
    returned = lax.all_to_all(expert_out, "req", split_axis=1, concat_axis=1, tiled=True)
    expert_row = returned.reshape(-1, width)[position].reshape(rows, choose_count, width)
    mix = jnp.einsum("rk,rkd->rd", gates, expert_row.astype(jnp.float32))
    return (hidden_state.astype(jnp.bfloat16), mix.astype(jnp.bfloat16))


def solution(mesh):
    body = on_places if mesh.shape["req"] == PLACES else on_slots
    return jax.shard_map(
        body,
        mesh=mesh,
        in_specs=(
            P("req", "tp"),
            P("tp", None),
            P(("req", "tp"), None),
            P(),
            P(),
            P(("req", "tp"), None),
            P("req", "tp", None),
            P("req", "tp", None),
            P("req", "tp", None),
        ),
        out_specs=(P(("req", "tp"), None), P(("req", "tp"), None)),
        check_vma=False,
    )
```

```python
import functools

import jax
import jax.numpy as jnp
from jax import lax
from jax.experimental import pallas as pl
from jax.experimental.pallas import tpu as pltpu
from jax.sharding import PartitionSpec as P

SWAP = [(0, 1), (1, 0)]
PLACES = 16
ACROSS_X = [(2 * i + t, 2 * (i ^ (1 + t)) + t) for i in range(PLACES) for t in range(2)]
ACROSS_Y = [(2 * i + t, 2 * (i ^ (2 - t)) + t) for i in range(PLACES) for t in range(2)]


def along_z(places):
    return [(2 * i + t, 2 * j + t) for i, j in places for t in range(2)]


PAIR_Z = along_z([(i, i ^ 4) for i in range(PLACES)])
MIDDLE_Z = along_z([(i, i ^ 12) for i in range(4, 12)])
OPPOSITE_Z = along_z([(i, i ^ 12) for i in range(PLACES)])
INWARD_Z = along_z([(i, i ^ 4) for i in (0, 1, 2, 3, 12, 13, 14, 15)])
OUTWARD_Z = along_z([(i, i ^ 4) for i in range(4, 12)])
NT = (((1,), (1,)), ((), ()))


def send(value, pairs):
    return lax.ppermute(value, ("req", "tp"), pairs)


def wide(value):
    return value.astype(jnp.float32)


def narrow(value):
    return value.astype(jnp.bfloat16)


def joined(*parts):
    return jnp.concatenate(parts, axis=0)


def together(*values):
    return lax.optimization_barrier(values)


def spread(own, weights):
    rows = own.shape[0]
    half = rows // 2
    z = lax.axis_index("req") // 4
    middle = (z == 1) | (z == 2)
    swapped = []

    def swap(value):
        swapped.append(lax.ppermute(value, "tp", SWAP))

    gate_w, up_w, down_w = weights
    swap(gate_w)
    own, up_w, swapped[0] = together(own, up_w, swapped[0])
    y0 = send(own, ACROSS_Y)
    x0 = send(own, ACROSS_X)
    pair = send(own, PAIR_Z)
    over = send(own, OPPOSITE_Z)
    swap(up_w)
    over, pair, x0, y0, swapped[1] = together(over, pair, x0, y0, swapped[1])
    to_x = joined(pair, y0[:half])
    to_y = joined(pair, x0[half:])
    over, pair, to_x, to_y, down_w = together(over, pair, to_x, to_y, down_w)
    out = send(over, OUTWARD_Z)
    next_ = send(pair, MIDDLE_Z)
    x1 = send(to_x, ACROSS_X)
    y1 = send(to_y, ACROSS_Y)
    swap(down_w)
    out, next_, x1, y1, swapped[2] = together(out, next_, x1, y1, swapped[2])
    far1 = jnp.where(middle, over, out)
    far2 = jnp.where(middle, next_, over)
    to_x = joined(far1, far2, y1[:half])
    to_y = joined(far1, far2, x1[half:rows])
    far1, far2, to_x, to_y = together(far1, far2, to_x, to_y)
    x2 = send(to_x, ACROSS_X)
    y2 = send(to_y, ACROSS_Y)
    return [own, x0, y0, pair, x1, y1], far1, far2, x2, y2, swapped


def spread_last(x2, y2, rows):
    half = rows // 2
    to_x = joined(y2[:half], y2[rows : rows + half])
    to_y = joined(x2[half:rows], x2[rows + half : 2 * rows])
    to_x, to_y = together(to_x, to_y)
    return send(to_x, ACROSS_X), send(to_y, ACROSS_Y)


def collect(first, second):
    own, x0, y0, pair, x1, y1 = first
    far1, far2, x_far1, x_far2, y_far1, y_far2, x3, y3 = second
    rows = own.shape[0]
    half = rows // 2

    def low(value, term):
        return joined(narrow(wide(value[:half]) + wide(term)), value[half:])

    def high(value, term):
        return joined(
            value[:half], narrow(wide(value[half:rows]) + wide(term)), value[rows:]
        )

    z = lax.axis_index("req") // 4
    middle = (z == 1) | (z == 2)
    by_x = send(x3, ACROSS_X)
    by_y = send(y3, ACROSS_Y)
    x_sum = send(high(x_far2, by_y[half:]), ACROSS_X)
    y_sum = send(low(y_far2, by_x[half:]), ACROSS_Y)
    x_far1, y_far1 = high(x_far1, by_y[:half]), low(y_far1, by_x[:half])
    x_far1, y_far1, x_sum, y_sum = together(x_far1, y_far1, x_sum, y_sum)
    next_ = send(narrow(wide(far2) + wide(x_sum) + wide(y_sum)), OPPOSITE_Z)
    x_sum = send(x_far1, ACROSS_X)
    y_sum = send(y_far1, ACROSS_Y)
    far1 = wide(far1) + wide(x_sum[:rows]) + wide(y_sum[:rows])
    inward = send(narrow(far1), INWARD_Z)
    near = send(narrow(far1 + wide(inward)), MIDDLE_Z)
    x_pair = send(high(x1, y_sum[rows:]), ACROSS_X)
    y_pair = send(low(y1, x_sum[rows:]), ACROSS_Y)
    pair = wide(pair) + wide(x_pair[:rows]) + wide(y_pair[:rows])
    pair = narrow(pair + jnp.where(middle, wide(next_), 0.0))
    by_pair = send(pair, PAIR_Z)
    x_own = send(high(x0, y_pair[rows:]), ACROSS_X)
    y_own = send(low(y0, x_pair[rows:]), ACROSS_Y)
    total = wide(own) + wide(x_own) + wide(y_own) + jnp.where(middle, 0.0, wide(next_))
    return total + wide(near) + wide(by_pair)


def expert_body(takes, gives, tile, group, loads, *refs):
    pieces = len({i for i, _, _ in takes})
    blocks, refs = refs[:pieces], refs[pieces:]
    if loads:
        router, local, gate_own, up_own, down_own, gate_far, up_far, down_far = refs[:8]
        outs, (ups, downs) = refs[8 : 8 + len(gives)], refs[8 + len(gives) :][:2]
        held, picks, spreads, sel, acts, up_sem, down_sem = refs[10 + len(gives) :]
    else:
        router, local, ups, downs = refs[:4]
        outs = refs[4 : 4 + len(gives)]
        held, picks, spreads, sel, acts = refs[4 + len(gives) :]
    total_rows, width = held.shape
    experts = router.shape[1]
    tiles = acts.shape[1]
    groups = total_rows // group
    slots = group // 2

    def up_copies(t):
        part = pl.ds(t * tile, tile)
        return [
            pltpu.make_async_copy(w.at[part, :], ups.at[i, t], up_sem.at[i, t])
            for i, w in enumerate((gate_own, up_own, gate_far, up_far))
        ]

    def down_copy(i):
        return pltpu.make_async_copy(
            (down_own, down_far)[i], downs.at[i], down_sem.at[i]
        )

    if loads:
        for t in range(tiles):
            for copy in up_copies(t):
                copy.start()
        for i in range(2):
            down_copy(i).start()
    at = 0
    for i, start, size in takes:
        held[at : at + size, :] = blocks[i][start : start + size, :width]
        picks[at : at + size, :] = blocks[i][start : start + size, width : width + 128]
        at += size
    for g in range(groups):
        part = slice(g * group, (g + 1) * group)
        x = held[part, :]
        pick = picks[part, :experts].astype(jnp.float32)
        logits = jnp.dot(x, router[...], preferred_element_type=jnp.float32)
        raised = jnp.where(pick > 0, jnp.exp(logits), 0.0)
        gate = raised / jnp.sum(raised, axis=1, keepdims=True)
        row = lax.broadcasted_iota(jnp.int32, (group, 1), 0)
        column = lax.broadcasted_iota(jnp.int32, (group, group), 1)
        chosen = jnp.zeros((group, group), jnp.float32)
        weighed = jnp.zeros((group, group), jnp.float32)
        for j in range(2):
            mine = local[j : j + 1, :]
            slot = jnp.sum(pick * mine, axis=1, keepdims=True).astype(jnp.int32)
            place = jnp.where(slot > 0, j * slots + row // 64 * 32 + slot - 1, -1)
            weight = jnp.sum(gate * mine, axis=1, keepdims=True)
            hit = column == place
            chosen = jnp.where(hit, 1.0, chosen)
            weighed = jnp.where(hit, weight, weighed)
        spreads[g] = weighed.astype(jnp.bfloat16)
        rows = jnp.dot(
            chosen.T.astype(jnp.bfloat16), x, preferred_element_type=jnp.float32
        ).astype(jnp.bfloat16)
        for j in range(2):
            sel[j, g * slots : (g + 1) * slots, :] = rows[j * slots : (j + 1) * slots, :]

    for t in range(tiles):
        if loads:
            for copy in up_copies(t):
                copy.wait()
        x = sel[t // (tiles // 2)]
        for i in range(2):
            h = lax.dot_general(x, ups[2 * i, t], NT, preferred_element_type=jnp.float32)
            u = lax.dot_general(
                x, ups[2 * i + 1, t], NT, preferred_element_type=jnp.float32
            )
            acts[i, t] = (h / (1.0 + jnp.exp(-h)) * u).astype(jnp.bfloat16)
    if loads:
        for i in range(2):
            down_copy(i).wait()

    def down(n, _):
        part = pl.ds(pl.multiple_of(n * tile, tile), tile)
        rows = []
        for j in range(2):
            total = None
            for t in range(j * tiles // 2, (j + 1) * tiles // 2):
                for i in range(2):
                    term = jnp.dot(
                        acts[i, t],
                        downs[i, t * tile : (t + 1) * tile, part],
                        preferred_element_type=jnp.float32,
                    )
                    total = term if total is None else total + term
            rows.append(total.astype(jnp.bfloat16))
        mixed = []
        for g in range(groups):
            slot_rows = jnp.concatenate(
                [r[g * slots : (g + 1) * slots, :] for r in rows], axis=0
            )
            mixed.append(
                jnp.dot(spreads[g], slot_rows, preferred_element_type=jnp.float32).astype(
                    jnp.bfloat16
                )
            )
        for out, ranges in zip(outs, gives):
            at = 0
            for start, size in ranges:
                g = start // group
                out[at : at + size, part] = mixed[g][start - g * group : start - g * group + size, :]
                at += size
        return 0

    lax.fori_loop(0, width // tile, down, 0, unroll=True)


def run_experts(blocks, takes, gives, router, local, weights, loads, tile=256, group=256):
    width = router.shape[0]
    if loads:
        hidden = weights[0].shape[0]
        tiles = hidden // tile
        copies = [
            pltpu.VMEM((4, tiles, tile, width), jnp.bfloat16),
            pltpu.VMEM((2, hidden, width), jnp.bfloat16),
        ]
    else:
        hidden = weights[1].shape[1]
        tiles = hidden // tile
        copies = []
        weights = [pltpu.with_memory_space_constraint(w, pltpu.VMEM) for w in weights]
    total_rows = sum(size for _, _, size in takes)
    sizes = [sum(size for _, size in ranges) for ranges in gives]
    vmem = pl.BlockSpec(memory_space=pltpu.VMEM)
    held_out = pl.BlockSpec(memory_space=pl.ANY)
    semaphores = [pltpu.SemaphoreType.DMA((4, tiles)), pltpu.SemaphoreType.DMA((2,))]
    return pl.pallas_call(
        functools.partial(expert_body, takes, gives, tile, group, loads),
        in_specs=[vmem] * (len(blocks) + 2) + [held_out if loads else vmem] * len(weights),
        out_specs=[vmem] * (len(sizes) + len(copies)),
        out_shape=[jax.ShapeDtypeStruct((size, width), jnp.bfloat16) for size in sizes]
        + copies,
        scratch_shapes=[
            pltpu.VMEM((total_rows, width), jnp.bfloat16),
            pltpu.VMEM((total_rows, 128), jnp.bfloat16),
            pltpu.VMEM((total_rows // group, group, group), jnp.bfloat16),
            pltpu.VMEM((2, total_rows // 2, width), jnp.bfloat16),
            pltpu.VMEM((2, tiles, total_rows // 2, tile), jnp.bfloat16),
        ]
        + (semaphores if loads else []),
        compiler_params=pltpu.CompilerParams(vmem_limit_bytes=24 * 1024 * 1024),
        cost_estimate=pl.CostEstimate(
            flops=8 * total_rows * width * hidden,
            bytes_accessed=12 * hidden * width + 4 * total_rows * width,
            transcendentals=total_rows * hidden,
        ),
    )(*blocks, router, local, *weights)


def project(attn, out_weight, stream_in, later):
    rows = stream_in.shape[0]
    me = lax.axis_index("tp")
    theirs = lax.dynamic_slice_in_dim(attn, (1 - me) * rows, rows, 0)
    ours = lax.dynamic_slice_in_dim(attn, me * rows, rows, 0)
    sent = jnp.dot(theirs, out_weight, preferred_element_type=jnp.float32)
    got = lax.ppermute(sent, "tp", SWAP)
    kept = jnp.dot(ours, out_weight, preferred_element_type=jnp.float32)
    got, later = lax.optimization_barrier((got, later))
    return stream_in.astype(jnp.float32) + (kept + got), later


def on_places(
    attn, out_weight, stream_in, norm_gain, router_weight, routes, gate_weight, up_weight, down_weight
):
    rows = stream_in.shape[0]
    half = rows // 2
    expert_count = router_weight.shape[1]
    experts = jnp.arange(expert_count, dtype=jnp.int32)
    me = lax.axis_index("req")
    named = jnp.any(routes[:, :, None] == experts, axis=1).astype(jnp.bfloat16)
    order = jnp.arange(rows)
    earlier = (order[None, :] <= order[:, None]).astype(jnp.bfloat16)
    slot = jnp.dot(earlier, named, preferred_element_type=jnp.float32)
    slot = (slot * named).astype(jnp.bfloat16)
    slot = jnp.pad(slot, ((0, 0), (0, 128 - expert_count)))
    local = (experts[None, :] == 2 * me + jnp.arange(2, dtype=jnp.int32)[:, None]).astype(
        jnp.float32
    )
    hidden_state, gate_weight = project(attn, out_weight, stream_in, gate_weight)
    scale = lax.rsqrt(jnp.mean(hidden_state * hidden_state, axis=1, keepdims=True) + 1e-06)
    normed = (hidden_state * scale * norm_gain).astype(jnp.bfloat16)
    width = stream_in.shape[1]
    weights = (gate_weight, up_weight, down_weight)
    own = tuple(w.reshape(-1, width) for w in weights)
    first, far1, far2, x2, y2, far = spread(jnp.concatenate([normed, slot], axis=1), weights)
    far = tuple(w.reshape(-1, width) for w in far)
    run = functools.partial(run_experts, router=router_weight, local=local)
    takes = tuple((i, 0, rows) for i in range(7)) + ((4, rows, half), (5, rows, half))
    gives = tuple(((i * rows, rows),) for i in range(4))
    gives += (((4 * rows, rows), (7 * rows, half)),)
    gives += (((5 * rows, rows), (7 * rows + half, half)),)
    gives += (((6 * rows, rows),),)
    *done, ups, downs = run(first + [far1], takes, gives, weights=(*own, *far), loads=True)
    x2, y2, *done = lax.optimization_barrier((x2, y2, *done))
    x3, y3 = spread_last(x2, y2, rows)
    first, (far1,) = done[:6], done[6:]
    takes = ((0, 0, 2 * rows), (1, 0, 2 * rows), (0, 2 * rows, half), (1, 2 * rows, half))
    takes += ((2, 0, half), (3, 0, half), (2, half, half), (3, half, half), (4, 0, rows))
    gives = (
        ((0, rows), (4 * rows, half)),
        ((rows, rows),),
        ((2 * rows, rows), (4 * rows + half, half)),
        ((3 * rows, rows),),
        ((5 * rows, half), (6 * rows, half)),
        ((5 * rows + half, half), (6 * rows + half, half)),
        ((7 * rows, rows),),
    )
    *second, far2 = run(
        [x2, y2, x3, y3, far2], takes, gives, weights=(ups, downs), loads=False
    )
    second = [far1, far2, *second]
    mix = collect(first, second)
    return (hidden_state.astype(jnp.bfloat16), mix.astype(jnp.bfloat16))


def slot_numbers(flat, count):
    onehot = (flat[:, None] == jnp.arange(count, dtype=jnp.int32)[None, :]).astype(jnp.int32)
    before = jnp.cumsum(onehot, axis=0) - onehot
    return jnp.sum(before * onehot, axis=1)


def swiglu_part(rows_in, gate_w, up_w, down_w):
    gate_h = jnp.einsum("ekd,efd->ekf", rows_in, gate_w, preferred_element_type=jnp.float32)
    up_h = jnp.einsum("ekd,efd->ekf", rows_in, up_w, preferred_element_type=jnp.float32)
    act = (jax.nn.silu(gate_h) * up_h).astype(jnp.bfloat16)
    return jnp.einsum("ekf,efd->ekd", act, down_w, preferred_element_type=jnp.float32)


def on_slots(
    attn, out_weight, stream_in, norm_gain, router_weight, routes, gate_weight, up_weight, down_weight
):
    rows, width = stream_in.shape
    hidden_state, _ = project(attn, out_weight, stream_in, gate_weight)
    scale = lax.rsqrt(jnp.mean(hidden_state * hidden_state, axis=1, keepdims=True) + 1e-06)
    normed = (hidden_state * scale * norm_gain).astype(jnp.bfloat16)
    expert_count = router_weight.shape[1]
    choose_count = routes.shape[1]
    local_experts = gate_weight.shape[0]
    req_count = lax.axis_size("req")
    capacity = 2 * rows * choose_count // expert_count
    logits = jnp.dot(normed, router_weight, preferred_element_type=jnp.float32)
    onehot = (
        routes[:, :, None] == jnp.arange(expert_count, dtype=jnp.int32)[None, None, :]
    ).astype(jnp.float32)
    picked = jnp.sum(onehot * logits[:, None, :], axis=2)
    raised = jnp.exp(picked)
    gates = raised / jnp.sum(raised, axis=1, keepdims=True)
    flat = routes.reshape(-1)
    slots = slot_numbers(flat, expert_count)
    position = (
        flat % local_experts * (req_count * capacity) + flat // local_experts * capacity + slots
    )
    source = jnp.arange(rows * choose_count, dtype=jnp.int32) // choose_count
    outgoing = (
        jnp.zeros((local_experts * req_count * capacity, width), jnp.bfloat16)
        .at[position]
        .set(normed[source])
    )
    outgoing = outgoing.reshape(local_experts, req_count * capacity, width)
    incoming = lax.all_to_all(outgoing, "req", split_axis=1, concat_axis=1, tiled=True)
    partial_out = swiglu_part(
        lax.all_gather(incoming, "tp", axis=1, tiled=True), gate_weight, up_weight, down_weight
    )
    expert_out = lax.psum_scatter(partial_out, "tp", scatter_dimension=1, tiled=True).astype(
        jnp.bfloat16
    )
    returned = lax.all_to_all(expert_out, "req", split_axis=1, concat_axis=1, tiled=True)
    expert_row = returned.reshape(-1, width)[position].reshape(rows, choose_count, width)
    mix = jnp.einsum("rk,rkd->rd", gates, expert_row.astype(jnp.float32))
    return (hidden_state.astype(jnp.bfloat16), mix.astype(jnp.bfloat16))


def solution(mesh):
    body = on_places if mesh.shape["req"] == PLACES else on_slots
    return jax.shard_map(
        body,
        mesh=mesh,
        in_specs=(
            P("req", "tp"),
            P("tp", None),
            P(("req", "tp"), None),
            P(),
            P(),
            P(("req", "tp"), None),
            P("req", "tp", None),
            P("req", "tp", None),
            P("req", "tp", None),
        ),
        out_specs=(P(("req", "tp"), None), P(("req", "tp"), None)),
        check_vma=False,
    )
```

```python
import functools

import jax
import jax.numpy as jnp
from jax import lax
from jax.experimental import pallas as pl
from jax.experimental.pallas import tpu as pltpu
from jax.sharding import PartitionSpec as P

SWAP = [(0, 1), (1, 0)]
PLACES = 16
ACROSS_X = [(2 * i + t, 2 * (i ^ (1 + t)) + t) for i in range(PLACES) for t in range(2)]
ACROSS_Y = [(2 * i + t, 2 * (i ^ (2 - t)) + t) for i in range(PLACES) for t in range(2)]


def along_z(places):
    return [(2 * i + t, 2 * j + t) for i, j in places for t in range(2)]


PAIR_Z = along_z([(i, i ^ 4) for i in range(PLACES)])
MIDDLE_Z = along_z([(i, i ^ 12) for i in range(4, 12)])
OPPOSITE_Z = along_z([(i, i ^ 12) for i in range(PLACES)])
INWARD_Z = along_z([(i, i ^ 4) for i in (0, 1, 2, 3, 12, 13, 14, 15)])
OUTWARD_Z = along_z([(i, i ^ 4) for i in range(4, 12)])
NT = (((1,), (1,)), ((), ()))


def send(value, pairs):
    return lax.ppermute(value, ("req", "tp"), pairs)


def wide(value):
    return value.astype(jnp.float32)


def narrow(value):
    return value.astype(jnp.bfloat16)


def joined(*parts):
    return jnp.concatenate(parts, axis=0)


def together(*values):
    return lax.optimization_barrier(values)


def spread(own, weights):
    rows = own.shape[0]
    half = rows // 2
    z = lax.axis_index("req") // 4
    middle = (z == 1) | (z == 2)
    swapped = []

    def swap(value):
        swapped.append(lax.ppermute(value, "tp", SWAP))

    gate_w, up_w, down_w = weights
    swap(gate_w)
    own, up_w, swapped[0] = together(own, up_w, swapped[0])
    y0 = send(own, ACROSS_Y)
    x0 = send(own, ACROSS_X)
    pair = send(own, PAIR_Z)
    over = send(own, OPPOSITE_Z)
    swap(up_w)
    over, pair, x0, y0, swapped[1] = together(over, pair, x0, y0, swapped[1])
    to_x = joined(pair, y0[:half])
    to_y = joined(pair, x0[half:])
    over, pair, to_x, to_y, down_w = together(over, pair, to_x, to_y, down_w)
    out = send(over, OUTWARD_Z)
    next_ = send(pair, MIDDLE_Z)
    x1 = send(to_x, ACROSS_X)
    y1 = send(to_y, ACROSS_Y)
    swap(down_w)
    out, next_, x1, y1, swapped[2] = together(out, next_, x1, y1, swapped[2])
    far1 = jnp.where(middle, over, out)
    far2 = jnp.where(middle, next_, over)
    to_x = joined(far1, far2, y1[:half])
    to_y = joined(far1, far2, x1[half:rows])
    far1, far2, to_x, to_y = together(far1, far2, to_x, to_y)
    x2 = send(to_x, ACROSS_X)
    y2 = send(to_y, ACROSS_Y)
    return [own, x0, y0, pair, x1, y1], far1, far2, x2, y2, swapped


def spread_last(x2, y2, rows):
    half = rows // 2
    to_x = joined(y2[:half], y2[rows : rows + half])
    to_y = joined(x2[half:rows], x2[rows + half : 2 * rows])
    to_x, to_y = together(to_x, to_y)
    return send(to_x, ACROSS_X), send(to_y, ACROSS_Y)


def collect(first, second):
    own, pair, far1, x1, x0, y1, y0, lo_x, lo_y = first
    x_far1, x_far2, y_far1, y_far2, x3, y3, far2 = second
    rows = own.shape[0]
    half = rows // 2
    z = lax.axis_index("req") // 4
    middle = (z == 1) | (z == 2)

    def low(value, term):
        return joined(narrow(wide(value[:half]) + wide(term)), value[half:])

    def high(value, term):
        return joined(
            value[:half], narrow(wide(value[half:rows]) + wide(term)), value[rows:]
        )

    by_x = send(x3, ACROSS_X)
    by_y = send(y3, ACROSS_Y)
    x_sum = send(high(x_far2, by_y[half:]), ACROSS_X)
    y_sum = send(low(y_far2, by_x[half:]), ACROSS_Y)
    x_far1, y_far1 = high(x_far1, by_y[:half]), low(y_far1, by_x[:half])
    x_far1, y_far1, x_sum, y_sum = together(x_far1, y_far1, x_sum, y_sum)
    to_x = joined(wide(x1) + wide(y_sum[rows:]), wide(x0) + wide(lo_y[:half]))
    to_y = joined(wide(y1) + wide(x_sum[rows:]), wide(y0) + wide(lo_x[:half]))
    far2 = wide(far2) + wide(x_sum[:rows]) + wide(y_sum[:rows])
    next_ = send(narrow(far2), OPPOSITE_Z)
    x_sum = send(x_far1, ACROSS_X)
    y_sum = send(y_far1, ACROSS_Y)
    to_x, to_y, next_ = together(narrow(to_x), narrow(to_y), next_)
    far1 = wide(far1) + wide(x_sum) + wide(y_sum)
    inward = send(narrow(far1), INWARD_Z)
    near = send(narrow(far1 + wide(inward)), MIDDLE_Z)
    hi_x = send(to_x, ACROSS_X)
    hi_y = send(to_y, ACROSS_Y)

    def halves(i):
        old, new = slice((i + 1) * half, (i + 2) * half), slice(i * half, (i + 1) * half)
        return joined(wide(lo_x[old]) + wide(hi_y[new]), wide(hi_x[new]) + wide(lo_y[old]))

    pair = wide(pair) + halves(0) + jnp.where(middle, wide(next_), 0.0)
    by_pair = send(narrow(pair), PAIR_Z)
    total = wide(own) + halves(1) + jnp.where(middle, 0.0, wide(next_))
    return total + wide(near) + wide(by_pair)


def expert_body(takes, gives, tile, group, loads, *refs):
    pieces = len({i for i, _, _ in takes})
    blocks, refs = refs[:pieces], refs[pieces:]
    if loads:
        router, local, gate_own, up_own, down_own, gate_far, up_far, down_far = refs[:8]
        outs, (ups, downs) = refs[8 : 8 + len(gives)], refs[8 + len(gives) :][:2]
        held, picks, spreads, sel, acts, up_sem, down_sem = refs[10 + len(gives) :]
    else:
        router, local, ups, downs = refs[:4]
        outs = refs[4 : 4 + len(gives)]
        held, picks, spreads, sel, acts = refs[4 + len(gives) :]
    total_rows, width = held.shape
    experts = router.shape[1]
    tiles = acts.shape[1]
    groups = total_rows // group
    slots = group // 2

    def up_copies(t):
        part = pl.ds(t * tile, tile)
        return [
            pltpu.make_async_copy(w.at[part, :], ups.at[i, t], up_sem.at[i, t])
            for i, w in enumerate((gate_own, up_own, gate_far, up_far))
        ]

    def down_copy(i):
        return pltpu.make_async_copy(
            (down_own, down_far)[i], downs.at[i], down_sem.at[i]
        )

    if loads:
        for t in range(tiles):
            for copy in up_copies(t):
                copy.start()
        for i in range(2):
            down_copy(i).start()
    at = 0
    for i, start, size in takes:
        held[at : at + size, :] = blocks[i][start : start + size, :width]
        picks[at : at + size, :] = blocks[i][start : start + size, width : width + 128]
        at += size
    for g in range(groups):
        part = slice(g * group, (g + 1) * group)
        x = held[part, :]
        pick = picks[part, :experts].astype(jnp.float32)
        logits = jnp.dot(x, router[...], preferred_element_type=jnp.float32)
        raised = jnp.where(pick > 0, jnp.exp(logits), 0.0)
        gate = raised / jnp.sum(raised, axis=1, keepdims=True)
        row = lax.broadcasted_iota(jnp.int32, (group, 1), 0)
        column = lax.broadcasted_iota(jnp.int32, (group, group), 1)
        chosen = jnp.zeros((group, group), jnp.float32)
        weighed = jnp.zeros((group, group), jnp.float32)
        for j in range(2):
            mine = local[j : j + 1, :]
            slot = jnp.sum(pick * mine, axis=1, keepdims=True).astype(jnp.int32)
            place = jnp.where(slot > 0, j * slots + row // 64 * 32 + slot - 1, -1)
            weight = jnp.sum(gate * mine, axis=1, keepdims=True)
            hit = column == place
            chosen = jnp.where(hit, 1.0, chosen)
            weighed = jnp.where(hit, weight, weighed)
        spreads[g] = weighed.astype(jnp.bfloat16)
        rows = jnp.dot(
            chosen.T.astype(jnp.bfloat16), x, preferred_element_type=jnp.float32
        ).astype(jnp.bfloat16)
        for j in range(2):
            sel[j, g * slots : (g + 1) * slots, :] = rows[j * slots : (j + 1) * slots, :]

    for t in range(tiles):
        if loads:
            for copy in up_copies(t):
                copy.wait()
        x = sel[t // (tiles // 2)]
        for i in range(2):
            h = lax.dot_general(x, ups[2 * i, t], NT, preferred_element_type=jnp.float32)
            u = lax.dot_general(
                x, ups[2 * i + 1, t], NT, preferred_element_type=jnp.float32
            )
            acts[i, t] = (h / (1.0 + jnp.exp(-h)) * u).astype(jnp.bfloat16)
    if loads:
        for i in range(2):
            down_copy(i).wait()

    def down(n, _):
        part = pl.ds(pl.multiple_of(n * tile, tile), tile)
        rows = []
        for j in range(2):
            total = None
            for t in range(j * tiles // 2, (j + 1) * tiles // 2):
                for i in range(2):
                    term = jnp.dot(
                        acts[i, t],
                        downs[i, t * tile : (t + 1) * tile, part],
                        preferred_element_type=jnp.float32,
                    )
                    total = term if total is None else total + term
            rows.append(total.astype(jnp.bfloat16))
        mixed = []
        for g in range(groups):
            slot_rows = jnp.concatenate(
                [r[g * slots : (g + 1) * slots, :] for r in rows], axis=0
            )
            mixed.append(
                jnp.dot(spreads[g], slot_rows, preferred_element_type=jnp.float32).astype(
                    jnp.bfloat16
                )
            )
        for out, ranges in zip(outs, gives):
            at = 0
            for start, size in ranges:
                g = start // group
                out[at : at + size, part] = mixed[g][start - g * group : start - g * group + size, :]
                at += size
        return 0

    lax.fori_loop(0, width // tile, down, 0, unroll=True)


def run_experts(blocks, takes, gives, router, local, weights, loads, tile=256, group=256):
    width = router.shape[0]
    if loads:
        hidden = weights[0].shape[0]
        tiles = hidden // tile
        copies = [
            pltpu.VMEM((4, tiles, tile, width), jnp.bfloat16),
            pltpu.VMEM((2, hidden, width), jnp.bfloat16),
        ]
    else:
        hidden = weights[1].shape[1]
        tiles = hidden // tile
        copies = []
        weights = [pltpu.with_memory_space_constraint(w, pltpu.VMEM) for w in weights]
    total_rows = sum(size for _, _, size in takes)
    sizes = [sum(size for _, size in ranges) for ranges in gives]
    vmem = pl.BlockSpec(memory_space=pltpu.VMEM)
    held_out = pl.BlockSpec(memory_space=pl.ANY)
    semaphores = [pltpu.SemaphoreType.DMA((4, tiles)), pltpu.SemaphoreType.DMA((2,))]
    return pl.pallas_call(
        functools.partial(expert_body, takes, gives, tile, group, loads),
        in_specs=[vmem] * (len(blocks) + 2) + [held_out if loads else vmem] * len(weights),
        out_specs=[vmem] * (len(sizes) + len(copies)),
        out_shape=[jax.ShapeDtypeStruct((size, width), jnp.bfloat16) for size in sizes]
        + copies,
        scratch_shapes=[
            pltpu.VMEM((total_rows, width), jnp.bfloat16),
            pltpu.VMEM((total_rows, 128), jnp.bfloat16),
            pltpu.VMEM((total_rows // group, group, group), jnp.bfloat16),
            pltpu.VMEM((2, total_rows // 2, width), jnp.bfloat16),
            pltpu.VMEM((2, tiles, total_rows // 2, tile), jnp.bfloat16),
        ]
        + (semaphores if loads else []),
        compiler_params=pltpu.CompilerParams(vmem_limit_bytes=24 * 1024 * 1024),
        cost_estimate=pl.CostEstimate(
            flops=8 * total_rows * width * hidden,
            bytes_accessed=12 * hidden * width + 4 * total_rows * width,
            transcendentals=total_rows * hidden,
        ),
    )(*blocks, router, local, *weights)


def project(attn, out_weight, stream_in, later):
    rows = stream_in.shape[0]
    me = lax.axis_index("tp")
    theirs = lax.dynamic_slice_in_dim(attn, (1 - me) * rows, rows, 0)
    ours = lax.dynamic_slice_in_dim(attn, me * rows, rows, 0)
    sent = jnp.dot(theirs, out_weight, preferred_element_type=jnp.float32)
    got = lax.ppermute(sent, "tp", SWAP)
    kept = jnp.dot(ours, out_weight, preferred_element_type=jnp.float32)
    got, later = lax.optimization_barrier((got, later))
    return stream_in.astype(jnp.float32) + (kept + got), later


def on_places(
    attn, out_weight, stream_in, norm_gain, router_weight, routes, gate_weight, up_weight, down_weight
):
    rows = stream_in.shape[0]
    half = rows // 2
    expert_count = router_weight.shape[1]
    experts = jnp.arange(expert_count, dtype=jnp.int32)
    me = lax.axis_index("req")
    named = jnp.any(routes[:, :, None] == experts, axis=1).astype(jnp.bfloat16)
    order = jnp.arange(rows)
    earlier = (order[None, :] <= order[:, None]).astype(jnp.bfloat16)
    slot = jnp.dot(earlier, named, preferred_element_type=jnp.float32)
    slot = (slot * named).astype(jnp.bfloat16)
    slot = jnp.pad(slot, ((0, 0), (0, 128 - expert_count)))
    local = (experts[None, :] == 2 * me + jnp.arange(2, dtype=jnp.int32)[:, None]).astype(
        jnp.float32
    )
    hidden_state, gate_weight = project(attn, out_weight, stream_in, gate_weight)
    scale = lax.rsqrt(jnp.mean(hidden_state * hidden_state, axis=1, keepdims=True) + 1e-06)
    normed = (hidden_state * scale * norm_gain).astype(jnp.bfloat16)
    width = stream_in.shape[1]
    weights = (gate_weight, up_weight, down_weight)
    own = tuple(w.reshape(-1, width) for w in weights)
    first, far1, far2, x2, y2, far = spread(jnp.concatenate([normed, slot], axis=1), weights)
    far = tuple(w.reshape(-1, width) for w in far)
    run = functools.partial(run_experts, router=router_weight, local=local)
    takes = tuple((i, 0, rows) for i in range(7)) + ((4, rows, half), (5, rows, half))

    def part(block, at):
        return (block * rows + at, half)

    gives = tuple(((i * rows, rows),) for i in (0, 3, 6))
    gives += ((part(4, half),), (part(1, half),), (part(5, 0),), (part(2, 0),))
    gives += ((part(7, 0), part(4, 0), part(1, 0)),)
    gives += ((part(7, half), part(5, half), part(2, half)),)
    *done, ups, downs = run(first + [far1], takes, gives, weights=(*own, *far), loads=True)
    x2, y2, *done = lax.optimization_barrier((x2, y2, *done))
    x3, y3 = spread_last(x2, y2, rows)
    *first, lo_x, lo_y = done
    lo_x = send(lo_x, ACROSS_X)
    lo_y = send(lo_y, ACROSS_Y)
    takes = ((0, 0, 2 * rows), (1, 0, 2 * rows), (0, 2 * rows, half), (1, 2 * rows, half))
    takes += ((2, 0, half), (3, 0, half), (2, half, half), (3, half, half), (4, 0, rows))
    gives = (
        ((0, rows),),
        ((rows, rows), part(4, 0)),
        ((2 * rows, rows),),
        ((3 * rows, rows), part(4, half)),
        (part(5, 0), part(6, 0)),
        (part(5, half), part(6, half)),
        ((7 * rows, rows),),
    )
    second = run(
        [x2, y2, x3, y3, far2], takes, gives, weights=(ups, downs), loads=False
    )
    lo_x, lo_y, *second = lax.optimization_barrier((lo_x, lo_y, *second))
    first = [*first, lo_x, lo_y]
    mix = collect(first, second)
    return (hidden_state.astype(jnp.bfloat16), mix.astype(jnp.bfloat16))


def slot_numbers(flat, count):
    onehot = (flat[:, None] == jnp.arange(count, dtype=jnp.int32)[None, :]).astype(jnp.int32)
    before = jnp.cumsum(onehot, axis=0) - onehot
    return jnp.sum(before * onehot, axis=1)


def swiglu_part(rows_in, gate_w, up_w, down_w):
    gate_h = jnp.einsum("ekd,efd->ekf", rows_in, gate_w, preferred_element_type=jnp.float32)
    up_h = jnp.einsum("ekd,efd->ekf", rows_in, up_w, preferred_element_type=jnp.float32)
    act = (jax.nn.silu(gate_h) * up_h).astype(jnp.bfloat16)
    return jnp.einsum("ekf,efd->ekd", act, down_w, preferred_element_type=jnp.float32)


def on_slots(
    attn, out_weight, stream_in, norm_gain, router_weight, routes, gate_weight, up_weight, down_weight
):
    rows, width = stream_in.shape
    hidden_state, _ = project(attn, out_weight, stream_in, gate_weight)
    scale = lax.rsqrt(jnp.mean(hidden_state * hidden_state, axis=1, keepdims=True) + 1e-06)
    normed = (hidden_state * scale * norm_gain).astype(jnp.bfloat16)
    expert_count = router_weight.shape[1]
    choose_count = routes.shape[1]
    local_experts = gate_weight.shape[0]
    req_count = lax.axis_size("req")
    capacity = 2 * rows * choose_count // expert_count
    logits = jnp.dot(normed, router_weight, preferred_element_type=jnp.float32)
    onehot = (
        routes[:, :, None] == jnp.arange(expert_count, dtype=jnp.int32)[None, None, :]
    ).astype(jnp.float32)
    picked = jnp.sum(onehot * logits[:, None, :], axis=2)
    raised = jnp.exp(picked)
    gates = raised / jnp.sum(raised, axis=1, keepdims=True)
    flat = routes.reshape(-1)
    slots = slot_numbers(flat, expert_count)
    position = (
        flat % local_experts * (req_count * capacity) + flat // local_experts * capacity + slots
    )
    source = jnp.arange(rows * choose_count, dtype=jnp.int32) // choose_count
    outgoing = (
        jnp.zeros((local_experts * req_count * capacity, width), jnp.bfloat16)
        .at[position]
        .set(normed[source])
    )
    outgoing = outgoing.reshape(local_experts, req_count * capacity, width)
    incoming = lax.all_to_all(outgoing, "req", split_axis=1, concat_axis=1, tiled=True)
    partial_out = swiglu_part(
        lax.all_gather(incoming, "tp", axis=1, tiled=True), gate_weight, up_weight, down_weight
    )
    expert_out = lax.psum_scatter(partial_out, "tp", scatter_dimension=1, tiled=True).astype(
        jnp.bfloat16
    )
    returned = lax.all_to_all(expert_out, "req", split_axis=1, concat_axis=1, tiled=True)
    expert_row = returned.reshape(-1, width)[position].reshape(rows, choose_count, width)
    mix = jnp.einsum("rk,rkd->rd", gates, expert_row.astype(jnp.float32))
    return (hidden_state.astype(jnp.bfloat16), mix.astype(jnp.bfloat16))


def solution(mesh):
    body = on_places if mesh.shape["req"] == PLACES else on_slots
    return jax.shard_map(
        body,
        mesh=mesh,
        in_specs=(
            P("req", "tp"),
            P("tp", None),
            P(("req", "tp"), None),
            P(),
            P(),
            P(("req", "tp"), None),
            P("req", "tp", None),
            P("req", "tp", None),
            P("req", "tp", None),
        ),
        out_specs=(P(("req", "tp"), None), P(("req", "tp"), None)),
        check_vma=False,
    )
```

```python
import functools

import jax
import jax.numpy as jnp
from jax import lax
from jax.experimental import pallas as pl
from jax.experimental.pallas import tpu as pltpu
from jax.sharding import PartitionSpec as P

SWAP = [(0, 1), (1, 0)]
PLACES = 16
ACROSS_X = [(2 * i + t, 2 * (i ^ (1 + t)) + t) for i in range(PLACES) for t in range(2)]
ACROSS_Y = [(2 * i + t, 2 * (i ^ (2 - t)) + t) for i in range(PLACES) for t in range(2)]


def along_z(places):
    return [(2 * i + t, 2 * j + t) for i, j in places for t in range(2)]


PAIR_Z = along_z([(i, i ^ 4) for i in range(PLACES)])
MIDDLE_Z = along_z([(i, i ^ 12) for i in range(4, 12)])
OPPOSITE_Z = along_z([(i, i ^ 12) for i in range(PLACES)])
INWARD_Z = along_z([(i, i ^ 4) for i in (0, 1, 2, 3, 12, 13, 14, 15)])
OUTWARD_Z = along_z([(i, i ^ 4) for i in range(4, 12)])
NT = (((1,), (1,)), ((), ()))


def send(value, pairs):
    return lax.ppermute(value, ("req", "tp"), pairs)


def wide(value):
    return value.astype(jnp.float32)


def narrow(value):
    return value.astype(jnp.bfloat16)


def joined(*parts):
    return jnp.concatenate(parts, axis=0)


def together(*values):
    return lax.optimization_barrier(values)


def spread(own, weights):
    rows = own.shape[0]
    half = rows // 2
    z = lax.axis_index("req") // 4
    middle = (z == 1) | (z == 2)
    swapped = []

    def swap(value):
        swapped.append(lax.ppermute(value, "tp", SWAP))

    gate_w, up_w, down_w = weights
    swap(gate_w)
    own, up_w, swapped[0] = together(own, up_w, swapped[0])
    y0 = send(own, ACROSS_Y)
    x0 = send(own, ACROSS_X)
    pair = send(own, PAIR_Z)
    over = send(own, OPPOSITE_Z)
    swap(up_w)
    over, pair, x0, y0, swapped[1] = together(over, pair, x0, y0, swapped[1])
    to_x = joined(pair, y0[:half])
    to_y = joined(pair, x0[half:])
    over, pair, to_x, to_y, down_w = together(over, pair, to_x, to_y, down_w)
    out = send(over, OUTWARD_Z)
    next_ = send(pair, MIDDLE_Z)
    x1 = send(to_x, ACROSS_X)
    y1 = send(to_y, ACROSS_Y)
    swap(down_w)
    out, next_, x1, y1, swapped[2] = together(out, next_, x1, y1, swapped[2])
    far1 = jnp.where(middle, over, out)
    far2 = jnp.where(middle, next_, over)
    to_x = joined(far1, far2, y1[:half])
    to_y = joined(far1, far2, x1[half:rows])
    far1, far2, to_x, to_y = together(far1, far2, to_x, to_y)
    x2 = send(to_x, ACROSS_X)
    y2 = send(to_y, ACROSS_Y)
    return [own, x0, y0, pair, x1, y1], far1, far2, x2, y2, swapped


def spread_last(x2, y2, rows):
    half = rows // 2
    to_x = joined(y2[:half], y2[rows : rows + half])
    to_y = joined(x2[half:rows], x2[rows + half : 2 * rows])
    to_x, to_y = together(to_x, to_y)
    return send(to_x, ACROSS_X), send(to_y, ACROSS_Y)


def collect(first, second):
    own, pair, far1, x1, x0, y1, y0, lo_x, lo_y = first
    x_far1, x_far2, y_far1, y_far2, x3, y3, far2 = second
    rows = own.shape[0]
    half = rows // 2
    z = lax.axis_index("req") // 4
    middle = (z == 1) | (z == 2)

    def low(value, term):
        return joined(narrow(wide(value[:half]) + wide(term)), value[half:])

    def high(value, term):
        return joined(
            value[:half], narrow(wide(value[half:rows]) + wide(term)), value[rows:]
        )

    by_x = send(x3, ACROSS_X)
    by_y = send(y3, ACROSS_Y)
    x_sum = send(high(x_far2, by_y[half:]), ACROSS_X)
    y_sum = send(low(y_far2, by_x[half:]), ACROSS_Y)
    x_far1, y_far1 = high(x_far1, by_y[:half]), low(y_far1, by_x[:half])
    x_far1, y_far1, x_sum, y_sum = together(x_far1, y_far1, x_sum, y_sum)
    to_x = joined(wide(x1) + wide(y_sum[rows:]), wide(x0) + wide(lo_y[:half]))
    to_y = joined(wide(y1) + wide(x_sum[rows:]), wide(y0) + wide(lo_x[:half]))
    far2 = wide(far2) + wide(x_sum[:rows]) + wide(y_sum[:rows])
    next_ = send(narrow(far2), OPPOSITE_Z)
    x_sum = send(x_far1, ACROSS_X)
    y_sum = send(y_far1, ACROSS_Y)
    to_x, to_y, next_ = together(narrow(to_x), narrow(to_y), next_)
    far1 = wide(far1) + wide(x_sum) + wide(y_sum)
    inward = send(narrow(far1), INWARD_Z)
    near = send(narrow(far1 + wide(inward)), MIDDLE_Z)
    hi_x = send(to_x, ACROSS_X)
    hi_y = send(to_y, ACROSS_Y)

    def halves(i):
        old, new = slice((i + 1) * half, (i + 2) * half), slice(i * half, (i + 1) * half)
        return joined(wide(lo_x[old]) + wide(hi_y[new]), wide(hi_x[new]) + wide(lo_y[old]))

    pair = wide(pair) + halves(0) + jnp.where(middle, wide(next_), 0.0)
    by_pair = send(narrow(pair), PAIR_Z)
    total = wide(own) + halves(1) + jnp.where(middle, 0.0, wide(next_))
    return total + wide(near) + wide(by_pair)


def expert_body(takes, gives, tile, group, loads, *refs):
    pieces = len({i for i, _, _ in takes})
    blocks, refs = refs[:pieces], refs[pieces:]
    if loads:
        router, local, gate_own, up_own, down_own, gate_far, up_far, down_far = refs[:8]
        outs, (ups, downs) = refs[8 : 8 + len(gives)], refs[8 + len(gives) :][:2]
        held, picks, spreads, sel, acts, up_sem, down_sem = refs[10 + len(gives) :]
    else:
        router, local, ups, downs = refs[:4]
        outs = refs[4 : 4 + len(gives)]
        held, picks, spreads, sel, acts = refs[4 + len(gives) :]
    total_rows, width = held.shape
    experts = router.shape[1]
    tiles = acts.shape[1]
    groups = total_rows // group
    slots = group // 2

    def up_copies(t):
        part = pl.ds(t * tile, tile)
        return [
            pltpu.make_async_copy(w.at[part, :], ups.at[i, t], up_sem.at[i, t])
            for i, w in enumerate((gate_own, up_own, gate_far, up_far))
        ]

    def down_copy(i):
        return pltpu.make_async_copy(
            (down_own, down_far)[i], downs.at[i], down_sem.at[i]
        )

    if loads:
        for t in range(tiles):
            for copy in up_copies(t):
                copy.start()
        for i in range(2):
            down_copy(i).start()
    at = 0
    for i, start, size in takes:
        held[at : at + size, :] = blocks[i][start : start + size, :width]
        picks[at : at + size, :] = blocks[i][start : start + size, width : width + 128]
        at += size
    for g in range(groups):
        part = slice(g * group, (g + 1) * group)
        x = held[part, :]
        pick = picks[part, :experts].astype(jnp.float32)
        logits = jnp.dot(x, router[...], preferred_element_type=jnp.float32)
        raised = jnp.where(pick > 0, jnp.exp(logits), 0.0)
        gate = raised / jnp.sum(raised, axis=1, keepdims=True)
        row = lax.broadcasted_iota(jnp.int32, (group, 1), 0)
        column = lax.broadcasted_iota(jnp.int32, (group, group), 1)
        chosen = jnp.zeros((group, group), jnp.float32)
        weighed = jnp.zeros((group, group), jnp.float32)
        for j in range(2):
            mine = local[j : j + 1, :]
            slot = jnp.sum(pick * mine, axis=1, keepdims=True).astype(jnp.int32)
            place = jnp.where(slot > 0, j * slots + row // 64 * 32 + slot - 1, -1)
            weight = jnp.sum(gate * mine, axis=1, keepdims=True)
            hit = column == place
            chosen = jnp.where(hit, 1.0, chosen)
            weighed = jnp.where(hit, weight, weighed)
        spreads[g] = weighed.astype(jnp.bfloat16)
        rows = jnp.dot(
            chosen.T.astype(jnp.bfloat16), x, preferred_element_type=jnp.float32
        ).astype(jnp.bfloat16)
        for j in range(2):
            sel[j, g * slots : (g + 1) * slots, :] = rows[j * slots : (j + 1) * slots, :]

    for t in range(tiles):
        if loads:
            for copy in up_copies(t):
                copy.wait()
        x = sel[t // (tiles // 2)]
        for i in range(2):
            h = lax.dot_general(x, ups[2 * i, t], NT, preferred_element_type=jnp.float32)
            u = lax.dot_general(
                x, ups[2 * i + 1, t], NT, preferred_element_type=jnp.float32
            )
            h = 0.5 * h
            acts[i, t] = ((h + h * jnp.tanh(h)) * u).astype(jnp.bfloat16)
    if loads:
        for i in range(2):
            down_copy(i).wait()

    def down(n, _):
        part = pl.ds(pl.multiple_of(n * tile, tile), tile)
        rows = []
        for j in range(2):
            total = None
            for t in range(j * tiles // 2, (j + 1) * tiles // 2):
                for i in range(2):
                    term = jnp.dot(
                        acts[i, t],
                        downs[i, t * tile : (t + 1) * tile, part],
                        preferred_element_type=jnp.float32,
                    )
                    total = term if total is None else total + term
            rows.append(total.astype(jnp.bfloat16))
        mixed = []
        for g in range(groups):
            slot_rows = jnp.concatenate(
                [r[g * slots : (g + 1) * slots, :] for r in rows], axis=0
            )
            mixed.append(
                jnp.dot(spreads[g], slot_rows, preferred_element_type=jnp.float32).astype(
                    jnp.bfloat16
                )
            )
        for out, ranges in zip(outs, gives):
            at = 0
            for start, size in ranges:
                g = start // group
                out[at : at + size, part] = mixed[g][start - g * group : start - g * group + size, :]
                at += size
        return 0

    lax.fori_loop(0, width // tile, down, 0, unroll=True)


def run_experts(blocks, takes, gives, router, local, weights, loads, tile=256, group=256):
    width = router.shape[0]
    if loads:
        hidden = weights[0].shape[0]
        tiles = hidden // tile
        copies = [
            pltpu.VMEM((4, tiles, tile, width), jnp.bfloat16),
            pltpu.VMEM((2, hidden, width), jnp.bfloat16),
        ]
    else:
        hidden = weights[1].shape[1]
        tiles = hidden // tile
        copies = []
        weights = [pltpu.with_memory_space_constraint(w, pltpu.VMEM) for w in weights]
    total_rows = sum(size for _, _, size in takes)
    sizes = [sum(size for _, size in ranges) for ranges in gives]
    vmem = pl.BlockSpec(memory_space=pltpu.VMEM)
    held_out = pl.BlockSpec(memory_space=pl.ANY)
    semaphores = [pltpu.SemaphoreType.DMA((4, tiles)), pltpu.SemaphoreType.DMA((2,))]
    return pl.pallas_call(
        functools.partial(expert_body, takes, gives, tile, group, loads),
        in_specs=[vmem] * (len(blocks) + 2) + [held_out if loads else vmem] * len(weights),
        out_specs=[vmem] * (len(sizes) + len(copies)),
        out_shape=[jax.ShapeDtypeStruct((size, width), jnp.bfloat16) for size in sizes]
        + copies,
        scratch_shapes=[
            pltpu.VMEM((total_rows, width), jnp.bfloat16),
            pltpu.VMEM((total_rows, 128), jnp.bfloat16),
            pltpu.VMEM((total_rows // group, group, group), jnp.bfloat16),
            pltpu.VMEM((2, total_rows // 2, width), jnp.bfloat16),
            pltpu.VMEM((2, tiles, total_rows // 2, tile), jnp.bfloat16),
        ]
        + (semaphores if loads else []),
        compiler_params=pltpu.CompilerParams(vmem_limit_bytes=24 * 1024 * 1024),
        cost_estimate=pl.CostEstimate(
            flops=8 * total_rows * width * hidden,
            bytes_accessed=12 * hidden * width + 4 * total_rows * width,
            transcendentals=total_rows * hidden,
        ),
    )(*blocks, router, local, *weights)


def project(attn, out_weight, stream_in, later):
    rows = stream_in.shape[0]
    me = lax.axis_index("tp")
    theirs = lax.dynamic_slice_in_dim(attn, (1 - me) * rows, rows, 0)
    ours = lax.dynamic_slice_in_dim(attn, me * rows, rows, 0)
    sent = jnp.dot(theirs, out_weight, preferred_element_type=jnp.float32)
    got = lax.ppermute(sent, "tp", SWAP)
    kept = jnp.dot(ours, out_weight, preferred_element_type=jnp.float32)
    got, later = lax.optimization_barrier((got, later))
    return stream_in.astype(jnp.float32) + (kept + got), later


def on_places(
    attn, out_weight, stream_in, norm_gain, router_weight, routes, gate_weight, up_weight, down_weight
):
    rows = stream_in.shape[0]
    half = rows // 2
    expert_count = router_weight.shape[1]
    experts = jnp.arange(expert_count, dtype=jnp.int32)
    me = lax.axis_index("req")
    named = jnp.any(routes[:, :, None] == experts, axis=1).astype(jnp.bfloat16)
    order = jnp.arange(rows)
    earlier = (order[None, :] <= order[:, None]).astype(jnp.bfloat16)
    slot = jnp.dot(earlier, named, preferred_element_type=jnp.float32)
    slot = (slot * named).astype(jnp.bfloat16)
    slot = jnp.pad(slot, ((0, 0), (0, 128 - expert_count)))
    local = (experts[None, :] == 2 * me + jnp.arange(2, dtype=jnp.int32)[:, None]).astype(
        jnp.float32
    )
    hidden_state, gate_weight = project(attn, out_weight, stream_in, gate_weight)
    scale = lax.rsqrt(jnp.mean(hidden_state * hidden_state, axis=1, keepdims=True) + 1e-06)
    normed = (hidden_state * scale * norm_gain).astype(jnp.bfloat16)
    width = stream_in.shape[1]
    weights = (gate_weight, up_weight, down_weight)
    own = tuple(w.reshape(-1, width) for w in weights)
    first, far1, far2, x2, y2, far = spread(jnp.concatenate([normed, slot], axis=1), weights)
    far = tuple(w.reshape(-1, width) for w in far)
    run = functools.partial(run_experts, router=router_weight, local=local)
    takes = tuple((i, 0, rows) for i in range(7)) + ((4, rows, half), (5, rows, half))

    def part(block, at):
        return (block * rows + at, half)

    gives = tuple(((i * rows, rows),) for i in (0, 3, 6))
    gives += ((part(4, half),), (part(1, half),), (part(5, 0),), (part(2, 0),))
    gives += ((part(7, 0), part(4, 0), part(1, 0)),)
    gives += ((part(7, half), part(5, half), part(2, half)),)
    *done, ups, downs = run(first + [far1], takes, gives, weights=(*own, *far), loads=True)
    x2, y2, *done = lax.optimization_barrier((x2, y2, *done))
    x3, y3 = spread_last(x2, y2, rows)
    *first, lo_x, lo_y = done
    lo_x = send(lo_x, ACROSS_X)
    lo_y = send(lo_y, ACROSS_Y)
    takes = ((0, 0, 2 * rows), (1, 0, 2 * rows), (0, 2 * rows, half), (1, 2 * rows, half))
    takes += ((2, 0, half), (3, 0, half), (2, half, half), (3, half, half), (4, 0, rows))
    gives = (
        ((0, rows),),
        ((rows, rows), part(4, 0)),
        ((2 * rows, rows),),
        ((3 * rows, rows), part(4, half)),
        (part(5, 0), part(6, 0)),
        (part(5, half), part(6, half)),
        ((7 * rows, rows),),
    )
    second = run(
        [x2, y2, x3, y3, far2], takes, gives, weights=(ups, downs), loads=False
    )
    lo_x, lo_y, *second = lax.optimization_barrier((lo_x, lo_y, *second))
    first = [*first, lo_x, lo_y]
    mix = collect(first, second)
    return (hidden_state.astype(jnp.bfloat16), mix.astype(jnp.bfloat16))


def slot_numbers(flat, count):
    onehot = (flat[:, None] == jnp.arange(count, dtype=jnp.int32)[None, :]).astype(jnp.int32)
    before = jnp.cumsum(onehot, axis=0) - onehot
    return jnp.sum(before * onehot, axis=1)


def swiglu_part(rows_in, gate_w, up_w, down_w):
    gate_h = jnp.einsum("ekd,efd->ekf", rows_in, gate_w, preferred_element_type=jnp.float32)
    up_h = jnp.einsum("ekd,efd->ekf", rows_in, up_w, preferred_element_type=jnp.float32)
    act = (jax.nn.silu(gate_h) * up_h).astype(jnp.bfloat16)
    return jnp.einsum("ekf,efd->ekd", act, down_w, preferred_element_type=jnp.float32)


def on_slots(
    attn, out_weight, stream_in, norm_gain, router_weight, routes, gate_weight, up_weight, down_weight
):
    rows, width = stream_in.shape
    hidden_state, _ = project(attn, out_weight, stream_in, gate_weight)
    scale = lax.rsqrt(jnp.mean(hidden_state * hidden_state, axis=1, keepdims=True) + 1e-06)
    normed = (hidden_state * scale * norm_gain).astype(jnp.bfloat16)
    expert_count = router_weight.shape[1]
    choose_count = routes.shape[1]
    local_experts = gate_weight.shape[0]
    req_count = lax.axis_size("req")
    capacity = 2 * rows * choose_count // expert_count
    logits = jnp.dot(normed, router_weight, preferred_element_type=jnp.float32)
    onehot = (
        routes[:, :, None] == jnp.arange(expert_count, dtype=jnp.int32)[None, None, :]
    ).astype(jnp.float32)
    picked = jnp.sum(onehot * logits[:, None, :], axis=2)
    raised = jnp.exp(picked)
    gates = raised / jnp.sum(raised, axis=1, keepdims=True)
    flat = routes.reshape(-1)
    slots = slot_numbers(flat, expert_count)
    position = (
        flat % local_experts * (req_count * capacity) + flat // local_experts * capacity + slots
    )
    source = jnp.arange(rows * choose_count, dtype=jnp.int32) // choose_count
    outgoing = (
        jnp.zeros((local_experts * req_count * capacity, width), jnp.bfloat16)
        .at[position]
        .set(normed[source])
    )
    outgoing = outgoing.reshape(local_experts, req_count * capacity, width)
    incoming = lax.all_to_all(outgoing, "req", split_axis=1, concat_axis=1, tiled=True)
    partial_out = swiglu_part(
        lax.all_gather(incoming, "tp", axis=1, tiled=True), gate_weight, up_weight, down_weight
    )
    expert_out = lax.psum_scatter(partial_out, "tp", scatter_dimension=1, tiled=True).astype(
        jnp.bfloat16
    )
    returned = lax.all_to_all(expert_out, "req", split_axis=1, concat_axis=1, tiled=True)
    expert_row = returned.reshape(-1, width)[position].reshape(rows, choose_count, width)
    mix = jnp.einsum("rk,rkd->rd", gates, expert_row.astype(jnp.float32))
    return (hidden_state.astype(jnp.bfloat16), mix.astype(jnp.bfloat16))


def solution(mesh):
    body = on_places if mesh.shape["req"] == PLACES else on_slots
    return jax.shard_map(
        body,
        mesh=mesh,
        in_specs=(
            P("req", "tp"),
            P("tp", None),
            P(("req", "tp"), None),
            P(),
            P(),
            P(("req", "tp"), None),
            P("req", "tp", None),
            P("req", "tp", None),
            P("req", "tp", None),
        ),
        out_specs=(P(("req", "tp"), None), P(("req", "tp"), None)),
        check_vma=False,
    )
```
